32 devices in a mesh: sec: 8 (over z, y), term: 4 (over x, core).
Axes of the slice: x: 2, y: 2, z: 4, core: 2. Of those that a mesh axis runs over, the one named last changes fastest.
Arguments:
- vector: bfloat16 [64, 2, 64, 1024], P('sec'), may hold values from -125 to 125
- right_sector: int32 [64, 2], P('sec'), may hold values from 0 to 63, as said below
- left_env: bfloat16 [64, 26, 4096], P('sec'), may hold values from -0.75 to 0.75
- right_env: bfloat16 [64, 26, 4096], P('sec'), may hold values from -0.21875 to 0.21875
- term_ops: bfloat16 [12, 8, 16, 16], P('term'), may hold values from -0.5 to 0.5
- term_left: int32 [12, 8], P('term'), may hold values from 0 to 25
- group_right: int32 [12], P('term'), may hold values from 0 to 25
Outputs:
- image_one: bfloat16 [64, 2, 64, 1024], P('sec', None, 'term')
- next_vector: bfloat16 [64, 2, 64, 1024], P('sec', None, 'term')
- image_two: bfloat16 [64, 2, 64, 1024], P('sec', None, 'term')
The draws below stay inside these ranges and needn't reach their ends.
Inputs may be any that keep to these rules, and one draw needn't show every extreme that they name: right_sector[p, j] is a right sector. For every two devices d and e of sec, exactly 2 of the blocks with p in [d * 8, (d + 1) * 8) have right sectors in [e * 8, (e + 1) * 8).
All inputs are finite; a program needn't handle non-finite values.
Results may differ from the reference program's by a relative error of at most 0.0081.
Values may be sent and summed in bfloat16 or wider, within the bound.
No kernel may reach another device: no remote copies, remote signals or barrier semaphores. Data moves between devices by JAX's collectives and lax.ppermute only.
A program may use at most 192 MiB of HBM per device.

```python
import jax
import jax.numpy as jnp
from jax import lax

P_SIZE = 16
DW = 26
BLK = 64
NQ = 2
SEC_DEV = 8
TERM_G = 8
SECTORS = 64
GROUPS = 12


def draw_right_sector(key, part):
    key_order, key_inner = jax.random.split(jax.random.fold_in(key, 11))
    devices_sec = SECTORS // SEC_DEV
    per_device = SEC_DEV * NQ
    device_keys = jax.random.split(key_order, devices_sec)
    orders = jax.vmap(lambda single: jax.random.permutation(single, per_device))(device_keys)
    target = orders % devices_sec
    inner = jax.random.randint(key_inner, (devices_sec, per_device), 0, SEC_DEV)
    sectors = target * SEC_DEV + inner
    return sectors.reshape(SECTORS, NQ).astype(jnp.int32)


def draw_vector(key, part):
    key_base, key_rows, key_cols = jax.random.split(jax.random.fold_in(key, 23), 3)
    shape = (SECTORS, NQ, BLK, P_SIZE * BLK)
    base = jnp.clip(jax.random.normal(key_base, shape, jnp.float32), -5.0, 5.0)
    row_scale = jnp.exp(jax.random.uniform(key_rows, (SECTORS, NQ, BLK, 1), jnp.float32, 0.0, 2.3))
    col_scale = jnp.exp(jax.random.uniform(key_cols, (SECTORS, NQ, 1, P_SIZE * BLK), jnp.float32, 0.0, 2.3))
    trend = 3.0 ** (jnp.arange(SECTORS, dtype=jnp.float32) / max(SECTORS - 1, 1))
    return (base * row_scale * col_scale * trend[:, None, None, None] / 12.0).astype(jnp.bfloat16)


def touch_ends(drawn, stream_key, smallest, top_value):
    longest = drawn.shape.index(max(drawn.shape))
    spots = []
    for shift in (0, 1):
        where = [jax.random.randint(jax.random.fold_in(stream_key, axis), (), 0, length) for axis, length in enumerate(drawn.shape)]
        where[longest] = (where[longest] + shift) % drawn.shape[longest]
        spots.append(tuple(where))
    return drawn.at[spots[0]].set(smallest).at[spots[1]].set(top_value)


def level_of(own_key, shape, cuts, least, largest):
    def one(dim, parts):
        steps = jax.random.uniform(jax.random.fold_in(jax.random.fold_in(own_key, 6), dim), (parts,), jnp.float32, least / len(cuts), largest / len(cuts))
        return jnp.repeat(jnp.exp(steps), shape[dim] // parts).reshape((-1,) + (1,) * (len(shape) - dim - 1))

    level = one(*cuts[0])
    for cut in cuts[1:]:
        level = level * one(*cut)
    return level


def centred(own_key, dims, scale, most, pieces=(), kind=jnp.bfloat16):
    result = scale * jax.random.normal(own_key, dims, jnp.float32)
    if pieces:
        result = result * level_of(own_key, dims, pieces, -0.22, 0.18)
    return jnp.clip(result, -most, most).astype(kind)


def setup_inputs(seed: int = 0) -> dict:
    key_of = jax.random.split(jax.random.key(seed), 8)
    return {
        "vector": draw_vector(jax.random.fold_in(key_of[7], 71), 0),
        "right_sector": draw_right_sector(jax.random.fold_in(key_of[7], 71), 0),
        "left_env": centred(key_of[2], (SECTORS, DW, BLK * BLK), BLK ** -0.5, 0.75, ((0, 8),)),
        "right_env": centred(key_of[3], (SECTORS, DW, BLK * BLK), (BLK * GROUPS) ** -0.5, 0.21875, ((0, 8),)),
        "term_ops": centred(key_of[4], (GROUPS, TERM_G, P_SIZE, P_SIZE), (P_SIZE * TERM_G) ** -0.5, 0.5, ((0, 4),)),
        "term_left": touch_ends(jax.random.randint(key_of[5], (GROUPS, TERM_G), 0, DW), jax.random.fold_in(key_of[5], 1), 0, DW - 1).astype(jnp.int32),
        "group_right": touch_ends(jax.random.randint(key_of[6], (GROUPS,), 0, DW), jax.random.fold_in(key_of[6], 1), 0, DW - 1).astype(jnp.int32),
    }


def apply_hamiltonian(vector, right_sector, left_env, right_env, term_ops, term_left, group_right):
    block_view = vector.reshape(SECTORS, NQ, BLK, P_SIZE, BLK).astype(jnp.float32)
    chosen_right = right_env[right_sector]

    def add_group(total, group_slot):
        operators = term_ops[group_slot].astype(jnp.float32)
        left_terms = term_left[group_slot]
        gathered = jnp.zeros((SECTORS, NQ, BLK, P_SIZE, BLK), jnp.float32)
        for position in range(TERM_G):
            left_matrix = jnp.take(left_env, left_terms[position], axis=1).reshape(SECTORS, BLK, BLK).astype(jnp.float32)
            contracted = jnp.einsum('pxl,pjlsr->pjxsr', left_matrix, block_view, precision=lax.Precision.HIGHEST)
            contracted = lax.optimization_barrier(contracted.astype(jnp.bfloat16)).astype(jnp.float32)
            gathered = gathered + jnp.einsum('ys,pjxsr->pjxyr', operators[position], contracted, precision=lax.Precision.HIGHEST)
        mixed_terms = lax.optimization_barrier(gathered.astype(jnp.bfloat16)).astype(jnp.float32)
        right_matrix = jnp.take(chosen_right, group_right[group_slot], axis=2).reshape(SECTORS, NQ, BLK, BLK).astype(jnp.float32)
        added = jnp.einsum('pjxyr,pjzr->pjxyz', mixed_terms, right_matrix, precision=lax.Precision.HIGHEST)
        return (total + added, None)
    start = jnp.zeros((SECTORS, NQ, BLK, P_SIZE, BLK), jnp.float32)
    total, _ = lax.scan(add_group, start, jnp.arange(GROUPS, dtype=jnp.int32))
    return total.astype(jnp.bfloat16).reshape(SECTORS, NQ, BLK, P_SIZE * BLK)

def reference(vector, right_sector, left_env, right_env, term_ops, term_left, group_right):
    image_one = apply_hamiltonian(vector, right_sector, left_env, right_env, term_ops, term_left, group_right)
    vector_f = vector.astype(jnp.float32)
    image_f = image_one.astype(jnp.float32)
    norm_sq = jnp.sum(vector_f * vector_f)
    correlation = jnp.sum(vector_f * image_f)
    ratio = correlation / norm_sq
    residual = image_f - ratio * vector_f
    residual_sq = jnp.sum(residual * residual)
    next_vector = (residual * jnp.sqrt(norm_sq / (residual_sq + 1e-06))).astype(jnp.bfloat16)
    image_two = apply_hamiltonian(next_vector, right_sector, left_env, right_env, term_ops, term_left, group_right)
    return (image_one, next_vector, image_two)
```

```python
import functools

import jax
import jax.numpy as jnp
from jax import lax
from jax.experimental import pallas as pl
from jax.experimental.pallas import tpu as pltpu
from jax.sharding import PartitionSpec as P

BF = jnp.bfloat16
F32 = jnp.float32
VMEM_LIMIT = 48 * 1024 * 1024


def low_half(shape):
    return lax.broadcasted_iota(jnp.int32, shape, len(shape) - 1) < shape[-1] // 2


def swap(tile):
    return pltpu.roll(tile, tile.shape[-1] // 2, 1)


def two_in_lanes(first, second):
    low = low_half(first.shape)
    return jnp.where(low, first, swap(second)), jnp.where(low, swap(first), second)


def fill_left(lhs, left_refs, wide):
    env_width = left_refs[0].shape[1]
    lane = 2 * wide
    depth = -(-env_width // 16) * 16
    lhs[...] = jnp.zeros_like(lhs)
    low = low_half((env_width, lane))
    for pair in range(wide // 2):
        for b, ref in enumerate(left_refs):
            tile = ref[0, :, pair * lane : (pair + 1) * lane].astype(F32)
            base = 2 * pair * depth
            cols = slice(b * lane, (b + 1) * lane)
            lhs[base : base + env_width, cols] = jnp.where(low, tile, 0.0).astype(BF)
            lhs[base + depth : base + depth + env_width, cols] = jnp.where(low, 0.0, tile).astype(BF)


def put_source(rhs, s, tile):
    rows, lane = tile.shape
    low = low_half(tile.shape)
    kept = (jnp.where(low, tile, 0.0).astype(BF), jnp.where(low, 0.0, tile).astype(BF))
    for b in range(2):
        for copy in range(2):
            base = (2 * b + copy) * rows
            rhs[base : base + rows, s * lane : (s + 1) * lane] = kept[b]


def contract_left(lhs, rhs, con, chunk=512):
    step = 256
    for n in range(rhs.shape[1] // step):
        cols = slice(n * step, (n + 1) * step)

        def one(i, carry):
            rows = pl.ds(pl.multiple_of(i * chunk, chunk), chunk)
            con[rows, cols] = jnp.dot(
                lhs[rows, :], rhs[:, cols], preferred_element_type=F32
            ).astype(BF)
            return carry

        lax.fori_loop(0, lhs.shape[0] // chunk, one, 0, unroll=True)


def mix(amat, con, mixed, phys, lane):
    depth = amat.shape[1] // phys
    groups = amat.shape[0] // phys
    pairs = con.shape[0] // depth // 2

    def one(pair, carry):
        halves = []
        for parity in range(2):
            rows = pl.ds(pl.multiple_of((2 * pair + parity) * depth, depth), depth)
            halves.append(
                jnp.concatenate(
                    [con[rows, s * lane : (s + 1) * lane] for s in range(phys)], axis=0
                )
            )
        out = jnp.dot(
            amat[...], jnp.concatenate(halves, axis=1), preferred_element_type=F32
        ).astype(BF)
        for parity in range(2):
            rows = pl.ds(pl.multiple_of((2 * pair + parity) * phys, phys), phys)
            for g in range(groups):
                mixed[rows, g * lane : (g + 1) * lane] = out[
                    g * phys : (g + 1) * phys, parity * lane : (parity + 1) * lane
                ]
        return carry

    lax.fori_loop(0, pairs, one, 0, unroll=2)


def fill_right(rmat, right_tiles, lane):
    for b, get in enumerate(right_tiles):
        wide = lane // 2
        rows = slice(b * wide, (b + 1) * wide)
        low = low_half((wide, lane))
        for pair in range(rmat.shape[1] // (2 * lane)):
            tile = get(pair).astype(F32)
            turned = swap(tile)
            if b == 0:
                first, second = jnp.where(low, tile, 0.0), jnp.where(low, turned, 0.0)
            else:
                first, second = jnp.where(low, 0.0, turned), jnp.where(low, 0.0, tile)
            rmat[rows, 2 * pair * lane : (2 * pair + 1) * lane] = first.astype(BF)
            rmat[rows, (2 * pair + 1) * lane : (2 * pair + 2) * lane] = second.astype(BF)


def contract_right(mixed, rmat, acc, chunk=256):
    for i in range(mixed.shape[0] // chunk):
        rows = slice(i * chunk, (i + 1) * chunk)
        acc[rows, :] = lax.dot_general(
            mixed[rows, :], rmat[...], (((1,), (1,)), ((), ())), preferred_element_type=F32
        )


def copy_operator(amat, parts):
    rows = amat.shape[0] // len(parts)
    for k, part in enumerate(parts):
        amat[k * rows : (k + 1) * rows, :] = part[:rows, :]


def left_kernel(parts_count, wide, phys, _, left_a, left_b, vec_a, vec_b, *refs):
    parts = refs[:parts_count]
    mixed, both, lhs, rhs, amat, con = refs[parts_count:]
    lane = 2 * wide
    copy_operator(amat, parts)
    fill_left(lhs, (left_a, left_b), wide)
    for pair in range(phys // 2):
        cols = slice(pair * lane, (pair + 1) * lane)
        tiles = two_in_lanes(vec_a[0, :, cols].astype(F32), vec_b[0, :, cols].astype(F32))
        for half, tile in enumerate(tiles):
            s = 2 * pair + half
            both[:, s * lane : (s + 1) * lane] = tile.astype(BF)
            put_source(rhs, s, tile)
    contract_left(lhs, rhs, con)
    mix(amat, con, mixed, phys, lane)


def split_rows(place, image, outs):
    terms = len(outs)
    rows = outs[0].shape[0]
    for k, out in enumerate(outs):
        quarter = lax.rem(place[0] + k, terms)
        out[...] = image[pl.ds(pl.multiple_of(quarter * rows, rows), rows), :]


def right_kernel(terms, kinds, wide, phys, place, mixed, both, *refs):
    rights = refs[: len(kinds)]
    image, stats = refs[len(kinds)], refs[len(kinds) + 1]
    outs = refs[len(kinds) + 2 : len(kinds) + 2 + terms]
    rmat, acc = refs[len(kinds) + 2 + terms :]
    lane = 2 * wide
    fill_right(
        rmat,
        [
            lambda pair, ref=ref, at=at: ref[at, :, pair * lane : (pair + 1) * lane]
            for ref, at in zip(rights, kinds)
        ],
        lane,
    )
    contract_right(mixed, rmat, acc)
    norm = jnp.zeros((wide, lane), F32)
    corr = jnp.zeros((wide, lane), F32)
    for y in range(phys):
        cols = slice(y * lane, (y + 1) * lane)
        tile = acc[pl.ds(y, wide, stride=phys), :].astype(BF)
        image[:, cols] = tile
        value = tile.astype(F32)
        vec = both[:, cols].astype(F32)
        norm += vec * vec
        corr += vec * value
    norm = jnp.sum(norm, keepdims=True)
    corr = jnp.sum(corr, keepdims=True)
    ratio = jnp.where(norm > 0, corr / jnp.where(norm > 0, norm, 1.0), 0.0)
    square = jnp.zeros((wide, lane), F32)
    cross = jnp.zeros((wide, lane), F32)
    for y in range(phys):
        cols = slice(y * lane, (y + 1) * lane)
        vec = both[:, cols].astype(F32)
        rest = image[:, cols].astype(F32) - ratio * vec
        square += rest * rest
        cross += rest * vec
    square = jnp.sum(square, keepdims=True)
    cross = jnp.sum(cross, keepdims=True)
    at = lax.broadcasted_iota(jnp.int32, stats.shape, 1)
    row = jnp.zeros(stats.shape, F32)
    for i, value in enumerate((norm, corr, ratio, square, cross)):
        row = jnp.where(at == i, value, row)
    stats[...] = row
    split_rows(place, image, outs)


def second_kernel(terms, kinds, wide, phys, place, scal, left_a, left_b, both, image, *refs):
    parts, refs = refs[:terms], refs[terms:]
    rights, refs = refs[: len(kinds)], refs[len(kinds) :]
    outs, refs = refs[:terms], refs[terms:]
    lhs, rhs, amat, con, mixed, rmat, acc, result = refs
    lane = 2 * wide
    copy_operator(amat, parts)
    fill_left(lhs, (left_a, left_b), wide)
    ratio, scale = scal[0], scal[1]
    for s in range(phys):
        cols = slice(s * lane, (s + 1) * lane)
        rest = image[:, cols].astype(F32) - ratio * both[:, cols].astype(F32)
        put_source(rhs, s, (rest * scale).astype(BF).astype(F32))
    contract_left(lhs, rhs, con)
    mix(amat, con, mixed, phys, lane)
    fill_right(
        rmat,
        [
            lambda pair, ref=ref, at=at: ref[at, :, pair * lane : (pair + 1) * lane]
            for ref, at in zip(rights, kinds)
        ],
        lane,
    )
    contract_right(mixed, rmat, acc)
    for y in range(phys):
        result[:, y * lane : (y + 1) * lane] = acc[pl.ds(y, wide, stride=phys), :].astype(BF)
    split_rows(place, result, outs)


def select_kernel(terms, wide, names, blocks, *refs):
    envs, outs = refs[: len(blocks)], refs[len(blocks) : -2]
    spread, rows_out = refs[-2:]
    env_width = envs[0].shape[1]
    lane = 2 * wide
    half = wide // 2
    groups = outs[0].shape[2] // wide
    local = groups // terms
    turn = names[groups]
    for env, (out, at) in zip(envs, blocks):
        for z in range(half):
            spread[pl.ds(z, env_width, stride=half), :] = env[
                0, :, z * lane : (z + 1) * lane
            ].astype(F32)

        def rows_of(g):
            k = lax.rem(turn + g // local, terms)
            name = names[k * local + g % local]
            return spread[pl.ds(pl.multiple_of(name * half, half), half), :]

        for pair in range(groups // 2):
            even, odd = two_in_lanes(rows_of(2 * pair), rows_of(2 * pair + 1))
            rows_out[pl.ds(0, half, stride=2), :] = even
            rows_out[pl.ds(1, half, stride=2), :] = odd
            outs[out][at, :, pair * lane : (pair + 1) * lane] = rows_out[...].astype(BF)


def place_kernel(terms, pairs, wide, phys, follows, table, *refs):
    if follows:
        scal, rows, refs = refs[0], refs[1], refs[2:]
    pieces, refs = refs[: terms * pairs], refs[terms * pairs :]
    out = refs[0]
    lane = 2 * wide
    slots = out.shape[0] // terms
    me = table[out.shape[0]]
    for k in range(terms):
        source = lax.rem(me + terms - k, terms)
        for pi in range(pairs):
            piece = pieces[k * pairs + pi]
            first = table[source * slots + 2 * pi]
            second = table[source * slots + 2 * pi + 1]
            for pair in range(phys // 2):
                cols = slice(pair * lane, (pair + 1) * lane)
                a, b = two_in_lanes(
                    piece[:, 2 * pair * lane : (2 * pair + 1) * lane].astype(F32),
                    piece[:, (2 * pair + 1) * lane : (2 * pair + 2) * lane].astype(F32),
                )
                out[first, :, cols] = a.astype(BF)
                out[second, :, cols] = b.astype(BF)
                if follows:
                    ratio, scale = scal[0], scal[1]
                    for where, value in ((first, a), (second, b)):
                        rest = value - ratio * rows[where, :, cols].astype(F32)
                        refs[1][where, :, cols] = (rest * scale).astype(BF)


def whole(shape):
    return pl.BlockSpec(shape, lambda *_: (0,) * len(shape))


def call(kernel, prefetch, in_specs, out_shapes, scratch, flops, moved):
    return pl.pallas_call(
        kernel,
        out_shape=out_shapes,
        grid_spec=pltpu.PrefetchScalarGridSpec(
            num_scalar_prefetch=prefetch,
            grid=(1,),
            in_specs=in_specs,
            out_specs=[whole(s.shape) for s in out_shapes],
            scratch_shapes=scratch,
        ),
        compiler_params=pltpu.CompilerParams(vmem_limit_bytes=VMEM_LIMIT),
        cost_estimate=pl.CostEstimate(flops=flops, bytes_accessed=moved, transcendentals=0),
    )


def body(vector, right_sector, left_env, right_env, term_ops, term_left, group_right):
    terms = lax.axis_size("term")
    secs = lax.axis_size("sec")
    per_device, per_left, wide, row_width = vector.shape
    phys = row_width // wide
    lane = 2 * wide
    blocks = per_device * per_left
    slots = blocks // terms
    pairs = slots // 2
    span = secs // terms
    each = blocks // secs
    env_width = left_env.shape[1]
    depth = -(-env_width // 16) * 16
    local = group_right.shape[0]
    groups = local * terms
    slab = wide // terms
    d = lax.axis_index("sec")
    me = lax.axis_index("term")
    both_axes = ("sec", "term")
    vec = vector.reshape(blocks, wide, row_width)

    flat = right_sector.reshape(blocks)
    dest = flat // per_device
    before = jnp.arange(blocks)[None, :] < jnp.arange(blocks)[:, None]
    rank = jnp.sum((dest[None, :] == dest[:, None]) & before, axis=1)
    turn = lax.rem(dest - d + secs, span)
    place = (dest // span) * slots + turn * each + rank
    hit = place[None, :] == jnp.arange(blocks)[:, None]
    order = jnp.sum(jnp.where(hit, jnp.arange(blocks)[None, :], 0), axis=1)
    by_place = jnp.sum(jnp.where(hit, (flat % per_device)[None, :], 0), axis=1)
    own = lax.dynamic_slice(order, (me * slots,), (slots,)).astype(jnp.int32)
    wanted = lax.dynamic_slice(by_place, (me * slots,), (slots,)).astype(jnp.int32)
    table = jnp.concatenate([order.astype(jnp.int32), me.reshape(1)])

    def partner(a, device, term):
        return (term * span + (a + device) % span) * terms + device // span

    asks = [
        [(dd * terms + t, partner(a, dd, t)) for dd in range(secs) for t in range(terms)]
        for a in range(span)
    ]
    asked = [
        lax.ppermute(wanted[a * each : (a + 1) * each], both_axes, asks[a]) for a in range(span)
    ]

    onehot = (term_left[:, :, None] == jnp.arange(depth)).astype(BF)
    operator = jnp.einsum(
        "gtys,gtw->gysw", term_ops, onehot, preferred_element_type=F32
    ).reshape(local * phys, phys * depth)
    names = jnp.pad(
        group_right.astype(F32)[None, :], ((0, 15), (0, phys * depth - local))
    )
    packed = jnp.concatenate([operator, names], axis=0).astype(BF)

    def shift(value, k):
        return lax.ppermute(value, "term", [(t, (t + k) % terms) for t in range(terms)])

    parts = [packed] + [shift(packed, k) for k in range(1, terms)]
    known = jnp.concatenate([p[local * phys, :local] for p in parts]).astype(jnp.int32)
    receiver = d // span
    names = jnp.concatenate([known, lax.rem(me - receiver + terms, terms).reshape(1)])
    asked = jnp.concatenate(asked)

    env_block = (1, env_width, wide * wide)
    right_shape = jax.ShapeDtypeStruct((each, wide, groups * wide), BF)
    chosen = call(
        functools.partial(
            lambda fn, names, asked, *refs: fn(names, *refs),
            lambda names, *refs: select_kernel(
                terms, wide, names, [(i // each, i % each) for i in range(slots)], *refs
            ),
        ),
        2,
        [
            pl.BlockSpec(env_block, lambda _, n, q, i=i: (q[i], 0, 0)) for i in range(slots)
        ],
        [right_shape] * span,
        [
            pltpu.VMEM((env_width * (wide // 2), lane), F32),
            pltpu.VMEM((wide, lane), F32),
        ],
        0,
        slots * env_width * wide * wide * 2,
    )(names, asked, *([right_env] * slots))
    rights = [
        lax.ppermute(chosen[a], both_axes, [(t, s) for s, t in asks[a]]) for a in range(span)
    ]

    rows = wide * depth
    left_flops = 2 * rows * 4 * wide * phys * lane
    mix_flops = 2 * groups * phys * phys * depth * wide * lane
    right_flops = 2 * wide * phys * groups * lane * lane
    part_shape = packed.shape
    mixed_shape = jax.ShapeDtypeStruct((wide * phys, groups * lane), BF)
    full_shape = jax.ShapeDtypeStruct((wide, phys * lane), BF)
    piece_shape = jax.ShapeDtypeStruct((slab, phys * lane), BF)
    con_scratch = [
        pltpu.VMEM((rows, 4 * wide), BF),
        pltpu.VMEM((4 * wide, phys * lane), BF),
        pltpu.VMEM((groups * phys, phys * depth), BF),
        pltpu.VMEM((rows, phys * lane), BF),
    ]
    right_scratch = [
        pltpu.VMEM((lane, groups * lane), BF),
        pltpu.VMEM((wide * phys, lane), F32),
    ]

    def left_specs(pi):
        return [
            pl.BlockSpec(
                env_block, lambda _, o, *s, i=i: (lax.div(o[i], per_left), 0, 0)
            )
            for i in (2 * pi, 2 * pi + 1)
        ]

    mixes = []
    for pi in range(pairs):
        mixes.append(
            call(
                functools.partial(left_kernel, terms, wide, phys),
                1,
                left_specs(pi)
                + [
                    pl.BlockSpec((1, wide, row_width), lambda _, o, i=i: (o[i], 0, 0))
                    for i in (2 * pi, 2 * pi + 1)
                ]
                + [whole(part_shape)] * terms,
                [mixed_shape, full_shape],
                con_scratch,
                left_flops + mix_flops,
                wide * phys * groups * lane * 2,
            )(own, left_env, left_env, vec, vec, *parts)
        )

    where = me.reshape(1).astype(jnp.int32)
    images, stats, pieces = [], [], []
    for pi in range(pairs):
        kinds = [(2 * pi) % each, (2 * pi + 1) % each]
        using = [rights[(2 * pi) // each], rights[(2 * pi + 1) // each]]
        image, stat, *outs = call(
            functools.partial(right_kernel, terms, kinds, wide, phys),
            1,
            [whole(mixed_shape.shape), whole(full_shape.shape)] + [whole(right_shape.shape)] * 2,
            [full_shape, jax.ShapeDtypeStruct((1, lane), F32)] + [piece_shape] * terms,
            right_scratch,
            right_flops,
            wide * phys * groups * lane * 2,
        )(where, *mixes[pi], *using)
        images.append(image)
        stats.append(stat)
        pieces.append(outs)

    def spread(pieces):
        return [
            pieces[pi][k] if k == 0 else shift(pieces[pi][k], k)
            for k in range(terms)
            for pi in range(pairs)
        ]

    first_pieces = spread(pieces)

    line = jnp.concatenate(stats, axis=0).reshape(1, pairs * lane)
    everyone = lax.all_to_all(
        jnp.broadcast_to(line, (secs * terms, pairs * lane)), both_axes, 0, 0, tiled=True
    ).reshape(secs * terms * pairs, lane)
    sums = [everyone[:, i] for i in range(5)]
    norm_sq = jnp.sum(sums[0])
    ratio = jnp.sum(sums[1]) / norm_sq
    off = sums[2] - ratio
    residual_sq = jnp.sum(sums[3] + 2 * off * sums[4] + off * off * sums[0])
    scal = jnp.stack([ratio, jnp.sqrt(norm_sq / (residual_sq + 1e-06))])

    smem = pl.BlockSpec(memory_space=pltpu.SMEM)
    pieces = []
    for pi in range(pairs):
        kinds = [(2 * pi) % each, (2 * pi + 1) % each]
        using = [rights[(2 * pi) // each], rights[(2 * pi + 1) // each]]
        pieces.append(
            call(
                functools.partial(
                    lambda fn, own, place, *refs: fn(place, *refs),
                    functools.partial(second_kernel, terms, kinds, wide, phys),
                ),
                2,
                [smem]
                + left_specs(pi)
                + [whole(full_shape.shape)] * 2
                + [whole(part_shape)] * terms
                + [whole(right_shape.shape)] * 2,
                [piece_shape] * terms,
                con_scratch
                + [pltpu.VMEM(mixed_shape.shape, BF)]
                + right_scratch
                + [pltpu.VMEM(full_shape.shape, BF)],
                left_flops + mix_flops + right_flops,
                4 * wide * phys * lane * 2,
            )(own, where, scal, left_env, left_env, mixes[pi][1], images[pi], *parts, *using)
        )
    second_pieces = spread(pieces)

    out_shape = jax.ShapeDtypeStruct((blocks, slab, row_width), BF)
    first_image, next_rows = call(
        functools.partial(place_kernel, terms, pairs, wide, phys, True),
        1,
        [smem, pl.BlockSpec((blocks, slab, row_width), lambda _, t: (0, t[blocks], 0))]
        + [whole(piece_shape.shape)] * (terms * pairs),
        [out_shape] * 2,
        [],
        0,
        blocks * slab * row_width * 8,
    )(table, scal, vec, *first_pieces)
    (second_image,) = call(
        functools.partial(place_kernel, terms, pairs, wide, phys, False),
        1,
        [whole(piece_shape.shape)] * (terms * pairs),
        [out_shape],
        [],
        0,
        blocks * slab * row_width * 4,
    )(table, *second_pieces)
    shape = (per_device, per_left, slab, row_width)
    return (first_image.reshape(shape), next_rows.reshape(shape), second_image.reshape(shape))


def solution(mesh):
    in_specs = (
        P("sec", None, None, None),
        P("sec", None),
        P("sec", None, None),
        P("sec", None, None),
        P("term", None, None, None),
        P("term", None),
        P("term"),
    )
    out_specs = (
        P("sec", None, "term", None),
        P("sec", None, "term", None),
        P("sec", None, "term", None),
    )
    return jax.shard_map(body, mesh=mesh, in_specs=in_specs, out_specs=out_specs, check_vma=False)
```

```python
import functools

import jax
import jax.numpy as jnp
from jax import lax
from jax.experimental import pallas as pl
from jax.experimental.pallas import tpu as pltpu
from jax.sharding import PartitionSpec as P

BF = jnp.bfloat16
F32 = jnp.float32
VMEM_LIMIT = 26 * 1024 * 1024


def low_half(shape):
    return lax.broadcasted_iota(jnp.int32, shape, len(shape) - 1) < shape[-1] // 2


def swap(tile):
    return pltpu.roll(tile, tile.shape[-1] // 2, 1)


def two_in_lanes(first, second):
    low = low_half(first.shape)
    return jnp.where(low, first, swap(second)), jnp.where(low, swap(first), second)


def fill_left(lhs, left_refs, wide):
    env_width = left_refs[0].shape[1]
    lane = 2 * wide
    depth = -(-env_width // 16) * 16
    lhs[...] = jnp.zeros_like(lhs)
    low = low_half((env_width, lane))
    for pair in range(wide // 2):
        for b, ref in enumerate(left_refs):
            tile = ref[0, :, pair * lane : (pair + 1) * lane].astype(F32)
            base = 2 * pair * depth
            cols = slice(b * lane, (b + 1) * lane)
            lhs[base : base + env_width, cols] = jnp.where(low, tile, 0.0).astype(BF)
            lhs[base + depth : base + depth + env_width, cols] = jnp.where(low, 0.0, tile).astype(BF)


def put_source(rhs, s, tile):
    rows, lane = tile.shape
    low = low_half(tile.shape)
    kept = (jnp.where(low, tile, 0.0).astype(BF), jnp.where(low, 0.0, tile).astype(BF))
    for b in range(2):
        for copy in range(2):
            base = (2 * b + copy) * rows
            rhs[base : base + rows, s * lane : (s + 1) * lane] = kept[b]


def contract_left(lhs, rhs, con, chunk=512):
    step = 256
    for n in range(rhs.shape[1] // step):
        cols = slice(n * step, (n + 1) * step)

        def one(i, carry):
            rows = pl.ds(pl.multiple_of(i * chunk, chunk), chunk)
            con[rows, cols] = jnp.dot(
                lhs[rows, :], rhs[:, cols], preferred_element_type=F32
            ).astype(BF)
            return carry

        lax.fori_loop(0, lhs.shape[0] // chunk, one, 0, unroll=True)


def mix(amat, con, mixed, phys, lane):
    depth = amat.shape[1] // phys
    groups = amat.shape[0] // phys
    pairs = con.shape[0] // depth // 2

    def one(pair, carry):
        halves = []
        for parity in range(2):
            rows = pl.ds(pl.multiple_of((2 * pair + parity) * depth, depth), depth)
            halves.append(
                jnp.concatenate(
                    [con[rows, s * lane : (s + 1) * lane] for s in range(phys)], axis=0
                )
            )
        out = jnp.dot(
            amat[...], jnp.concatenate(halves, axis=1), preferred_element_type=F32
        ).astype(BF)
        for parity in range(2):
            rows = pl.ds(pl.multiple_of((2 * pair + parity) * phys, phys), phys)
            for g in range(groups):
                mixed[rows, g * lane : (g + 1) * lane] = out[
                    g * phys : (g + 1) * phys, parity * lane : (parity + 1) * lane
                ]
        return carry

    lax.fori_loop(0, pairs, one, 0, unroll=8)


def fill_right(rmat, right_tiles, lane):
    for b, get in enumerate(right_tiles):
        wide = lane // 2
        rows = slice(b * wide, (b + 1) * wide)
        low = low_half((wide, lane))
        for pair in range(rmat.shape[1] // (2 * lane)):
            tile = get(pair).astype(F32)
            turned = swap(tile)
            if b == 0:
                first, second = jnp.where(low, tile, 0.0), jnp.where(low, turned, 0.0)
            else:
                first, second = jnp.where(low, 0.0, turned), jnp.where(low, 0.0, tile)
            rmat[rows, 2 * pair * lane : (2 * pair + 1) * lane] = first.astype(BF)
            rmat[rows, (2 * pair + 1) * lane : (2 * pair + 2) * lane] = second.astype(BF)


def contract_right(mixed, rmat, acc, chunk=256):
    for i in range(mixed.shape[0] // chunk):
        rows = slice(i * chunk, (i + 1) * chunk)
        acc[rows, :] = lax.dot_general(
            mixed[rows, :], rmat[...], (((1,), (1,)), ((), ())), preferred_element_type=F32
        )


def copy_operator(amat, parts):
    rows = amat.shape[0] // len(parts)
    for k, part in enumerate(parts):
        amat[k * rows : (k + 1) * rows, :] = part[:rows, :]


def left_kernel(parts_count, wide, phys, _, left_a, left_b, vec_a, vec_b, *refs):
    parts = refs[:parts_count]
    mixed, both, lhs, rhs, amat, con = refs[parts_count:]
    mixed, both = mixed.at[0], both.at[0]
    lane = 2 * wide
    copy_operator(amat, parts)
    fill_left(lhs, (left_a, left_b), wide)
    for pair in range(phys // 2):
        cols = slice(pair * lane, (pair + 1) * lane)
        tiles = two_in_lanes(vec_a[0, :, cols].astype(F32), vec_b[0, :, cols].astype(F32))
        for half, tile in enumerate(tiles):
            s = 2 * pair + half
            both[:, s * lane : (s + 1) * lane] = tile.astype(BF)
            put_source(rhs, s, tile)
    contract_left(lhs, rhs, con)
    mix(amat, con, mixed, phys, lane)


def split_rows(place, image, outs):
    terms = len(outs)
    rows = outs[0].shape[0]
    for k, out in enumerate(outs):
        quarter = lax.rem(place[0] + k, terms)
        out[...] = image[pl.ds(pl.multiple_of(quarter * rows, rows), rows), :]


def right_kernel(terms, kinds, wide, phys, place, mixes, boths, *refs):
    pairs = len(kinds)
    count = len({at for pair in kinds for at, _ in pair})
    rights, refs = refs[:count], refs[count:]
    images, line = refs[:2]
    outs, (rmat, acc) = refs[2 : 2 + terms], refs[2 + terms :]
    lane = 2 * wide
    for pi in range(pairs):
        mixed, both, image = mixes.at[pi], boths.at[pi], images.at[pi]
        fill_right(rmat, tiles_of(rights, kinds[pi], lane), lane)
        contract_right(mixed, rmat, acc)
        norm = jnp.zeros((wide, lane), F32)
        corr = jnp.zeros((wide, lane), F32)
        for y in range(phys):
            cols = slice(y * lane, (y + 1) * lane)
            tile = acc[pl.ds(y, wide, stride=phys), :].astype(BF)
            image[:, cols] = tile
            value = tile.astype(F32)
            vec = both[:, cols].astype(F32)
            norm += vec * vec
            corr += vec * value
        norm = jnp.sum(norm, keepdims=True)
        corr = jnp.sum(corr, keepdims=True)
        ratio = jnp.where(norm > 0, corr / jnp.where(norm > 0, norm, 1.0), 0.0)
        square = jnp.zeros((wide, lane), F32)
        cross = jnp.zeros((wide, lane), F32)
        for y in range(phys):
            cols = slice(y * lane, (y + 1) * lane)
            vec = both[:, cols].astype(F32)
            rest = image[:, cols].astype(F32) - ratio * vec
            square += rest * rest
            cross += rest * vec
        square = jnp.sum(square, keepdims=True)
        cross = jnp.sum(cross, keepdims=True)
        at = lax.broadcasted_iota(jnp.int32, (1, lane), 1)
        row = jnp.zeros((1, lane), F32)
        for i, value in enumerate((norm, corr, ratio, square, cross)):
            row = jnp.where(at == i, value, row)
        line[:, :, pi * lane : (pi + 1) * lane] = jnp.broadcast_to(
            row[None], (line.shape[0], 1, lane)
        )
        split_rows(place, image, [out.at[pi] for out in outs])


def tiles_of(rights, kind, lane):
    return [
        lambda pair, ref=rights[array], at=at: ref[at, :, pair * lane : (pair + 1) * lane]
        for array, at in kind
    ]


def scalars(everyone):
    norm, corr, own, square, cross = (everyone[:, i : i + 1] for i in range(5))
    norm_sq = jnp.sum(norm, keepdims=True)
    ratio = jnp.sum(corr, keepdims=True) / norm_sq
    off = own - ratio
    residual_sq = jnp.sum(square + 2 * off * cross + off * off * norm, keepdims=True)
    return ratio, jnp.sqrt(norm_sq / (residual_sq + 1e-06))


def second_kernel(terms, kinds, wide, phys, place, scal, left_a, left_b, both, image, *refs):
    both, image = both.at[0], image.at[0]
    parts, refs = refs[:terms], refs[terms:]
    rights, refs = refs[:2], refs[2:]
    outs, refs = refs[:terms], refs[terms:]
    lhs, rhs, amat, con, mixed, rmat, acc, result = refs
    lane = 2 * wide
    copy_operator(amat, parts)
    fill_left(lhs, (left_a, left_b), wide)
    ratio, scale = scalars(scal)
    for s in range(phys):
        cols = slice(s * lane, (s + 1) * lane)
        rest = image[:, cols].astype(F32) - ratio * both[:, cols].astype(F32)
        put_source(rhs, s, (rest * scale).astype(BF).astype(F32))
    contract_left(lhs, rhs, con)
    mix(amat, con, mixed, phys, lane)
    fill_right(rmat, tiles_of(rights, kinds, lane), lane)
    contract_right(mixed, rmat, acc)
    for y in range(phys):
        result[:, y * lane : (y + 1) * lane] = acc[pl.ds(y, wide, stride=phys), :].astype(BF)
    split_rows(place, result, outs)


def select_kernel(wide, names, blocks, *refs):
    envs, outs = refs[: len(blocks)], refs[len(blocks) : -2]
    spread, rows_out = refs[-2:]
    env_width = envs[0].shape[1]
    lane = 2 * wide
    half = wide // 2
    groups = outs[0].shape[2] // wide
    for env, (out, at) in zip(envs, blocks):
        for z in range(half):
            tile = env[0, :, z * lane : (z + 1) * lane].astype(F32)
            for top in range(0, env_width, 8):
                part = tile[top : top + 8]
                base = top * half + z * 8
                spread[base : base + part.shape[0], :] = part

        def rows_of(g):
            name = names[g]
            return spread[pl.ds((name // 8) * (8 * half) + name % 8, half, stride=8), :]

        for pair in range(groups // 2):
            even, odd = two_in_lanes(rows_of(2 * pair), rows_of(2 * pair + 1))
            rows_out[pl.ds(0, half, stride=2), :] = even
            rows_out[pl.ds(1, half, stride=2), :] = odd
            outs[out][at, :, pair * lane : (pair + 1) * lane] = rows_out[...].astype(BF)


def place_kernel(terms, pairs, wide, phys, follows, table, *refs):
    if follows:
        scal, rows, refs = refs[0], refs[1], refs[2:]
        ratio, scale = scalars(scal)
    count = terms if follows else terms * pairs
    pieces, refs = refs[:count], refs[count:]
    out = refs[0]
    lane = 2 * wide
    slots = out.shape[0] // terms
    me = table[out.shape[0]]
    for k in range(terms):
        source = lax.rem(me + terms - k, terms)
        for pi in range(pairs):
            piece = pieces[k].at[pi] if follows else pieces[k * pairs + pi]
            first = table[source * slots + 2 * pi]
            second = table[source * slots + 2 * pi + 1]
            for pair in range(phys // 2):
                cols = slice(pair * lane, (pair + 1) * lane)
                a, b = two_in_lanes(
                    piece[:, 2 * pair * lane : (2 * pair + 1) * lane].astype(F32),
                    piece[:, (2 * pair + 1) * lane : (2 * pair + 2) * lane].astype(F32),
                )
                out[first, :, cols] = a.astype(BF)
                out[second, :, cols] = b.astype(BF)
                if follows:
                    for where, value in ((first, a), (second, b)):
                        rest = value - ratio * rows[where, :, cols].astype(F32)
                        refs[1][where, :, cols] = (rest * scale).astype(BF)


def whole(shape):
    return pl.BlockSpec(shape, lambda *_: (0,) * len(shape))


def call(kernel, prefetch, in_specs, out_shapes, scratch, flops, moved, grid=1, out_specs=None):
    return pl.pallas_call(
        kernel,
        out_shape=out_shapes,
        grid_spec=pltpu.PrefetchScalarGridSpec(
            num_scalar_prefetch=prefetch,
            grid=(grid,),
            in_specs=in_specs,
            out_specs=out_specs or [whole(s.shape) for s in out_shapes],
            scratch_shapes=scratch,
        ),
        compiler_params=pltpu.CompilerParams(vmem_limit_bytes=VMEM_LIMIT),
        cost_estimate=pl.CostEstimate(flops=flops, bytes_accessed=moved, transcendentals=0),
    )


def body(vector, right_sector, left_env, right_env, term_ops, term_left, group_right):
    terms = lax.axis_size("term")
    secs = lax.axis_size("sec")
    per_device, per_left, wide, row_width = vector.shape
    phys = row_width // wide
    lane = 2 * wide
    blocks = per_device * per_left
    slots = blocks // terms
    pairs = slots // 2
    span = secs // terms
    each = blocks // secs
    env_width = left_env.shape[1]
    depth = -(-env_width // 16) * 16
    local = group_right.shape[0]
    groups = local * terms
    slab = wide // terms
    d = lax.axis_index("sec")
    me = lax.axis_index("term")
    both_axes = ("sec", "term")
    vec = vector.reshape(blocks, wide, row_width)

    lines = terms // 2

    def flip(t, a):
        return (t % 2 * span + a) * lines + t // 2

    flat = right_sector.reshape(blocks)
    dest = flat // per_device
    before = jnp.arange(blocks)[None, :] < jnp.arange(blocks)[:, None]
    rank = jnp.sum((dest[None, :] == dest[:, None]) & before, axis=1)
    flips = dest ^ d
    column = flips // lines
    place = (flips % lines * 2 + column // span) * slots + column % span * each + rank
    hit = place[None, :] == jnp.arange(blocks)[:, None]
    order = jnp.sum(jnp.where(hit, jnp.arange(blocks)[None, :], 0), axis=1)
    by_place = jnp.sum(jnp.where(hit, (flat % per_device)[None, :], 0), axis=1)
    own = lax.dynamic_slice(order, (me * slots,), (slots,)).astype(jnp.int32)
    wanted = lax.dynamic_slice(by_place, (me * slots,), (slots,)).astype(jnp.int32)
    table = jnp.concatenate([order.astype(jnp.int32), me.reshape(1)])

    swaps = [
        [(e * terms + t, (e ^ flip(t, a)) * terms + t) for e in range(secs) for t in range(terms)]
        for a in range(span)
    ]
    asked = [
        lax.ppermute(wanted[a * each : (a + 1) * each], both_axes, swaps[a]) for a in range(span)
    ]

    onehot = (term_left[:, :, None] == jnp.arange(depth)).astype(BF)
    operator = jnp.einsum(
        "gtys,gtw->gysw", term_ops, onehot, preferred_element_type=F32
    ).reshape(local * phys, phys * depth)
    names = jnp.pad(
        group_right.astype(F32)[None, :], ((0, 15), (0, phys * depth - local))
    )
    packed = jnp.concatenate([operator, names], axis=0).astype(BF)

    def shift(value, k):
        return lax.ppermute(value, "term", [(t, (t + k) % terms) for t in range(terms)])

    parts = [packed] + [shift(packed, k) for k in range(1, terms)]
    known = jnp.concatenate([p[local * phys, :local] for p in parts]).astype(jnp.int32)
    asked = jnp.concatenate(asked)

    env_block = (1, env_width, wide * wide)
    right_shape = jax.ShapeDtypeStruct((each, wide, groups * wide), BF)
    chosen = call(
        functools.partial(
            lambda fn, names, asked, *refs: fn(names, *refs),
            lambda names, *refs: select_kernel(
                wide, names, [(i // each, i % each) for i in range(slots)], *refs
            ),
        ),
        2,
        [
            pl.BlockSpec(env_block, lambda _, n, q, i=i: (q[i], 0, 0)) for i in range(slots)
        ],
        [right_shape] * span,
        [
            pltpu.VMEM((-(-env_width // 8) * 8 * (wide // 2), lane), F32),
            pltpu.VMEM((wide, lane), F32),
        ],
        0,
        slots * env_width * wide * wide * 2,
    )(known, asked, *([right_env] * slots))
    rights = [lax.ppermute(chosen[a], both_axes, swaps[a]) for a in range(span)]

    rows = wide * depth
    left_flops = 2 * rows * 4 * wide * phys * lane
    mix_flops = 2 * groups * phys * phys * depth * wide * lane
    right_flops = 2 * wide * phys * groups * lane * lane
    part_shape = packed.shape
    mixed_shape = jax.ShapeDtypeStruct((wide * phys, groups * lane), BF)
    full_shape = jax.ShapeDtypeStruct((wide, phys * lane), BF)
    piece_shape = jax.ShapeDtypeStruct((slab, phys * lane), BF)
    con_scratch = [
        pltpu.VMEM((rows, 4 * wide), BF),
        pltpu.VMEM((4 * wide, phys * lane), BF),
        pltpu.VMEM((groups * phys, phys * depth), BF),
        pltpu.VMEM((rows, phys * lane), BF),
    ]
    right_scratch = [
        pltpu.VMEM((lane, groups * lane), BF),
        pltpu.VMEM((wide * phys, lane), F32),
    ]

    def left_specs(pi):
        return [
            pl.BlockSpec(
                env_block, lambda _, o, *s, i=i: (lax.div(o[i], per_left), 0, 0)
            )
            for i in (2 * pi, 2 * pi + 1)
        ]

    def of_pair(shape):
        return pl.BlockSpec((1, *shape), lambda i, *_: (i, *(0,) * len(shape)))

    def stacked(shape):
        return jax.ShapeDtypeStruct((pairs, *shape.shape), shape.dtype)

    mixes, boths = call(
        functools.partial(left_kernel, terms, wide, phys),
        1,
        [
            pl.BlockSpec(env_block, lambda i, o, b=b: (lax.div(o[2 * i + b], per_left), 0, 0))
            for b in range(2)
        ]
        + [
            pl.BlockSpec((1, wide, row_width), lambda i, o, b=b: (o[2 * i + b], 0, 0))
            for b in range(2)
        ]
        + [whole(part_shape)] * terms,
        [stacked(mixed_shape), stacked(full_shape)],
        con_scratch,
        pairs * (left_flops + mix_flops),
        pairs * wide * phys * groups * lane * 2,
        pairs,
        [of_pair(mixed_shape.shape), of_pair(full_shape.shape)],
    )(own, left_env, left_env, vec, vec, *parts)

    where = me.reshape(1).astype(jnp.int32)
    kinds = [[((2 * pi + b) // each, (2 * pi + b) % each) for b in range(2)] for pi in range(pairs)]
    images, line, *pieces = call(
        functools.partial(right_kernel, terms, kinds, wide, phys),
        1,
        [whole((pairs, *mixed_shape.shape)), whole((pairs, *full_shape.shape))]
        + [whole(right_shape.shape)] * span,
        [stacked(full_shape), jax.ShapeDtypeStruct((secs * terms, 1, pairs * lane), F32)]
        + [stacked(piece_shape)] * terms,
        right_scratch,
        pairs * right_flops,
        pairs * wide * phys * groups * lane * 2,
    )(where, mixes, boths, *rights)

    everyone = lax.all_to_all(line, both_axes, 0, 0, tiled=True).reshape(-1, lane)
    pieces, everyone = lax.optimization_barrier((pieces, everyone))
    first_pieces = [pieces[0]] + [shift(pieces[k], k) for k in range(1, terms)]

    sums_spec = whole(everyone.shape)
    second_pieces = [None] * (terms * pairs)
    sums = everyone
    for pi in range(pairs):
        if pi == pairs - 1:
            first_pieces, sums = lax.optimization_barrier((first_pieces, sums))
        one_pair = pl.BlockSpec((1, *full_shape.shape), lambda *_, pi=pi: (pi, 0, 0))
        outs = call(
            functools.partial(
                lambda fn, own, place, *refs: fn(place, *refs),
                functools.partial(
                    second_kernel, terms, [(b, at) for b, (_, at) in enumerate(kinds[pi])], wide, phys
                ),
            ),
            2,
            [sums_spec]
            + left_specs(pi)
            + [one_pair] * 2
            + [whole(part_shape)] * terms
            + [whole(right_shape.shape)] * 2,
            [piece_shape] * terms,
            con_scratch
            + [pltpu.VMEM(mixed_shape.shape, BF)]
            + right_scratch
            + [pltpu.VMEM(full_shape.shape, BF)],
            left_flops + mix_flops + right_flops,
            4 * wide * phys * lane * 2,
        )(
            own, where, sums, left_env, left_env, boths, images, *parts,
            *(rights[array] for array, _ in kinds[pi]),
        )
        for k, out in enumerate(outs):
            second_pieces[k * pairs + pi] = out if k == 0 else shift(out, k)

    out_shape = jax.ShapeDtypeStruct((blocks, slab, row_width), BF)
    first_image, next_rows = call(
        functools.partial(place_kernel, terms, pairs, wide, phys, True),
        1,
        [sums_spec, pl.BlockSpec((blocks, slab, row_width), lambda _, t: (0, t[blocks], 0))]
        + [whole((pairs, *piece_shape.shape))] * terms,
        [out_shape] * 2,
        [],
        0,
        blocks * slab * row_width * 8,
    )(table, everyone, vec, *first_pieces)
    (second_image,) = call(
        functools.partial(place_kernel, terms, pairs, wide, phys, False),
        1,
        [whole(piece_shape.shape)] * (terms * pairs),
        [out_shape],
        [],
        0,
        blocks * slab * row_width * 4,
    )(table, *second_pieces)
    shape = (per_device, per_left, slab, row_width)
    return (first_image.reshape(shape), next_rows.reshape(shape), second_image.reshape(shape))


def solution(mesh):
    in_specs = (
        P("sec", None, None, None),
        P("sec", None),
        P("sec", None, None),
        P("sec", None, None),
        P("term", None, None, None),
        P("term", None),
        P("term"),
    )
    out_specs = (
        P("sec", None, "term", None),
        P("sec", None, "term", None),
        P("sec", None, "term", None),
    )
    return jax.shard_map(body, mesh=mesh, in_specs=in_specs, out_specs=out_specs, check_vma=False)
```

```python
import functools

import jax
import jax.numpy as jnp
from jax import lax
from jax.experimental import pallas as pl
from jax.experimental.pallas import tpu as pltpu
from jax.sharding import PartitionSpec as P

BF = jnp.bfloat16
F32 = jnp.float32
SUMS = 5
VMEM_LIMIT = 26 * 1024 * 1024


def low_half(shape):
    return lax.broadcasted_iota(jnp.int32, shape, len(shape) - 1) < shape[-1] // 2


def swap(tile):
    return pltpu.roll(tile, tile.shape[-1] // 2, 1)


def two_in_lanes(first, second):
    low = low_half(first.shape)
    return jnp.where(low, first, swap(second)), jnp.where(low, swap(first), second)


def fill_left(lhs, left_refs, wide):
    env_width = left_refs[0].shape[0]
    lane = 2 * wide
    depth = -(-env_width // 16) * 16
    lhs[...] = jnp.zeros_like(lhs)
    low = low_half((env_width, lane))
    for pair in range(wide // 2):
        for b, ref in enumerate(left_refs):
            tile = ref[:, pair * lane : (pair + 1) * lane].astype(F32)
            base = 2 * pair * depth
            cols = slice(b * lane, (b + 1) * lane)
            lhs[base : base + env_width, cols] = jnp.where(low, tile, 0.0).astype(BF)
            lhs[base + depth : base + depth + env_width, cols] = jnp.where(low, 0.0, tile).astype(BF)


def put_source(rhs, s, tile):
    rows, lane = tile.shape
    low = low_half(tile.shape)
    kept = (jnp.where(low, tile, 0.0).astype(BF), jnp.where(low, 0.0, tile).astype(BF))
    for b in range(2):
        for copy in range(2):
            base = (2 * b + copy) * rows
            rhs[base : base + rows, s * lane : (s + 1) * lane] = kept[b]


def contract_left(lhs, rhs, con, chunk=512):
    step = 256
    for n in range(rhs.shape[1] // step):
        cols = slice(n * step, (n + 1) * step)

        def one(i, carry):
            rows = pl.ds(pl.multiple_of(i * chunk, chunk), chunk)
            con[rows, cols] = jnp.dot(
                lhs[rows, :], rhs[:, cols], preferred_element_type=F32
            ).astype(BF)
            return carry

        lax.fori_loop(0, lhs.shape[0] // chunk, one, 0, unroll=True)


def mix(amat, con, mixed, phys, lane):
    depth = amat.shape[1] // phys
    groups = amat.shape[0] // phys
    pairs = con.shape[0] // depth // 2

    def one(pair, carry):
        halves = []
        for parity in range(2):
            rows = pl.ds(pl.multiple_of((2 * pair + parity) * depth, depth), depth)
            halves.append(
                jnp.concatenate(
                    [con[rows, s * lane : (s + 1) * lane] for s in range(phys)], axis=0
                )
            )
        out = jnp.dot(
            amat[...], jnp.concatenate(halves, axis=1), preferred_element_type=F32
        ).astype(BF)
        for parity in range(2):
            rows = pl.ds(pl.multiple_of((2 * pair + parity) * phys, phys), phys)
            for g in range(groups):
                mixed[rows, g * lane : (g + 1) * lane] = out[
                    g * phys : (g + 1) * phys, parity * lane : (parity + 1) * lane
                ]
        return carry

    lax.fori_loop(0, pairs, one, 0, unroll=True)


def fill_right(rmat, right_tiles, lane):
    for b, get in enumerate(right_tiles):
        wide = lane // 2
        rows = slice(b * wide, (b + 1) * wide)
        low = low_half((wide, lane))
        for pair in range(rmat.shape[1] // (2 * lane)):
            tile = get(pair).astype(F32)
            turned = swap(tile)
            if b == 0:
                first, second = jnp.where(low, tile, 0.0), jnp.where(low, turned, 0.0)
            else:
                first, second = jnp.where(low, 0.0, turned), jnp.where(low, 0.0, tile)
            rmat[rows, 2 * pair * lane : (2 * pair + 1) * lane] = first.astype(BF)
            rmat[rows, (2 * pair + 1) * lane : (2 * pair + 2) * lane] = second.astype(BF)


def contract_right(mixed, rmat, acc, chunk=256):
    for i in range(mixed.shape[0] // chunk):
        rows = slice(i * chunk, (i + 1) * chunk)
        acc[rows, :] = lax.dot_general(
            mixed[rows, :], rmat[...], (((1,), (1,)), ((), ())), preferred_element_type=F32
        )


def copy_operator(amat, parts):
    rows = amat.shape[0] // len(parts)
    for k, part in enumerate(parts):
        amat[k * rows : (k + 1) * rows, :] = part[:rows, :]


def left_kernel(per_left, wide, phys, own, left_env, vec, *refs):
    parts = refs[:-6]
    mixes, boths, lefts, amat, rhs, con = refs[-6:]
    lane = 2 * wide
    copy_operator(amat, parts)

    def one(pi, carry):
        first, second = own[2 * pi], own[2 * pi + 1]
        both, lhs = boths.at[pi], lefts.at[pi]
        fill_left(lhs, [left_env.at[lax.div(n, per_left)] for n in (first, second)], wide)
        for pair in range(phys // 2):
            cols = slice(pair * lane, (pair + 1) * lane)
            tiles = two_in_lanes(vec[first, :, cols].astype(F32), vec[second, :, cols].astype(F32))
            for half, tile in enumerate(tiles):
                s = 2 * pair + half
                both[:, s * lane : (s + 1) * lane] = tile.astype(BF)
                put_source(rhs, s, tile)
        contract_left(lhs, rhs, con)
        mix(amat, con, mixes.at[pi], phys, lane)
        return carry

    lax.fori_loop(0, boths.shape[0], one, 0)


def quarter_of(place, k, rows):
    return pl.multiple_of(lax.bitwise_xor(place[0], k) * rows, rows)


def right_kernel(terms, kinds, wide, phys, place, mixes, boths, *refs):
    pairs = len(kinds)
    count = len({at for pair in kinds for at, _ in pair})
    rights, refs = refs[:count], refs[count:]
    images, line, rmats = refs[:3]
    outs, accs = refs[3 : 3 + terms], refs[3 + terms]
    lane = 2 * wide
    slab = wide // terms
    at = lax.broadcasted_iota(jnp.int32, (1, lane), 1)
    row = jnp.zeros((1, lane), F32)
    for pi in range(pairs):
        both, image = boths.at[pi], images.at[pi]
        fill_right(rmats.at[pi], tiles_of(rights, kinds[pi], lane), lane)
        acc = accs.at[pi]
        contract_right(mixes.at[pi], rmats.at[pi], acc)
        norm = jnp.zeros((wide, lane), F32)
        corr = jnp.zeros((wide, lane), F32)
        for y in range(phys):
            cols = slice(y * lane, (y + 1) * lane)
            tile = acc[pl.ds(y, wide, stride=phys), :].astype(BF)
            image[:, cols] = tile
            value = tile.astype(F32)
            vec = both[:, cols].astype(F32)
            norm += vec * vec
            corr += vec * value
        norm = jnp.sum(norm, keepdims=True)
        corr = jnp.sum(corr, keepdims=True)
        ratio = jnp.where(norm > 0, corr / jnp.where(norm > 0, norm, 1.0), 0.0)
        square = jnp.zeros((wide, lane), F32)
        cross = jnp.zeros((wide, lane), F32)
        for y in range(phys):
            cols = slice(y * lane, (y + 1) * lane)
            vec = both[:, cols].astype(F32)
            rest = image[:, cols].astype(F32) - ratio * vec
            square += rest * rest
            cross += rest * vec
        square = jnp.sum(square, keepdims=True)
        cross = jnp.sum(cross, keepdims=True)
        for i, value in enumerate((norm, corr, ratio, square, cross)):
            row = jnp.where(at == SUMS * pi + i, value, row)
        for k, out in enumerate(outs):
            out[pi] = image[pl.ds(quarter_of(place, k, slab), slab), :]
    line[...] = jnp.broadcast_to(row[None], line.shape)


def tiles_of(rights, kind, lane):
    return [
        lambda pair, ref=rights[array], at=at: ref[at, :, pair * lane : (pair + 1) * lane]
        for array, at in kind
    ]


def scalars(everyone, pairs):
    def all_of(i):
        return [everyone[:, SUMS * pi + i : SUMS * pi + i + 1] for pi in range(pairs)]

    def total(columns):
        return jnp.sum(functools.reduce(jnp.add, columns), keepdims=True)

    norm_sq = total(all_of(0))
    ratio = total(all_of(1)) / norm_sq
    rests = []
    for norm, own, square, cross in zip(*(all_of(i) for i in (0, 2, 3, 4))):
        off = own - ratio
        rests.append(square + 2 * off * cross + off * off * norm)
    return ratio, jnp.sqrt(norm_sq / (total(rests) + 1e-06))


def second_kernel(terms, pi, wide, phys, place, everyone, boths, images, lefts, amat, rmats, *refs):
    carried = refs[:terms] if pi == 0 else ()
    outs = refs[len(carried) : len(carried) + terms]
    rhs, con, mixed, acc = refs[len(carried) + terms :]
    lane = 2 * wide
    slab = wide // terms
    ratio, scale = scalars(everyone, boths.shape[0])
    for s in range(phys):
        cols = slice(s * lane, (s + 1) * lane)
        rest = images[pi, :, cols].astype(F32) - ratio * boths[pi, :, cols].astype(F32)
        put_source(rhs, s, (rest * scale).astype(BF).astype(F32))
    contract_left(lefts.at[pi], rhs, con)
    mix(amat, con, mixed, phys, lane)
    contract_right(mixed, rmats.at[pi], acc)
    for k, out in enumerate(outs):
        last = out.shape[0] - 1
        if carried:
            out[:last] = carried[k][...]
        base = quarter_of(place, k, slab) * phys
        for y in range(phys):
            out[last, :, y * lane : (y + 1) * lane] = acc[
                pl.ds(base + y, slab, stride=phys), :
            ].astype(BF)


def select_kernel(wide, blocks, names, asked, right_env, *refs):
    outs = refs[:-2]
    spread, rows_out = refs[-2:]
    env_width = right_env.shape[1]
    lane = 2 * wide
    half = wide // 2
    groups = outs[0].shape[2] // wide
    for i, (out, at) in enumerate(blocks):
        env = right_env.at[asked[i]]
        for z in range(half):
            tile = env[:, z * lane : (z + 1) * lane].astype(F32)
            for top in range(0, env_width, 8):
                part = tile[top : top + 8]
                base = top * half + z * 8
                spread[base : base + part.shape[0], :] = part

        def rows_of(g):
            name = names[g]
            return spread[pl.ds((name // 8) * (8 * half) + name % 8, half, stride=8), :]

        for pair in range(groups // 2):
            even, odd = two_in_lanes(rows_of(2 * pair), rows_of(2 * pair + 1))
            rows_out[pl.ds(0, half, stride=2), :] = even
            rows_out[pl.ds(1, half, stride=2), :] = odd
            outs[out][at, :, pair * lane : (pair + 1) * lane] = rows_out[...].astype(BF)


def place_kernel(terms, wide, phys, count, follows, table, *refs):
    if follows:
        ratio, scale = scalars(refs[0], count)
        vec, refs = refs[1], refs[2:]
        out, following = refs[-2:]
    else:
        out = refs[-1]
    lane = 2 * wide
    blocks, slab, _ = out.shape
    slots = blocks // terms
    me = table[blocks]
    for k in range(terms):
        source = lax.bitwise_xor(me, k)
        for pi in range(count):
            if follows:
                piece = refs[k].at[pi]
            elif pi == 0:
                piece = refs[k].at[count]
            else:
                piece = refs[terms * pi + k].at[0]
            first = table[source * slots + 2 * pi]
            second = table[source * slots + 2 * pi + 1]
            for pair in range(phys // 2):
                cols = slice(pair * lane, (pair + 1) * lane)
                both = two_in_lanes(
                    piece[:, 2 * pair * lane : (2 * pair + 1) * lane].astype(F32),
                    piece[:, (2 * pair + 1) * lane : (2 * pair + 2) * lane].astype(F32),
                )
                for where, value in zip((first, second), both):
                    out[where, :, cols] = value.astype(BF)
                    if follows:
                        rows = pl.ds(pl.multiple_of(me * slab, slab), slab)
                        rest = value - ratio * vec[where, rows, cols].astype(F32)
                        following[where, :, cols] = (rest * scale).astype(BF)


def call(kernel, tables, operands, out_shapes, scratch, flops, moved):
    specs = [
        pl.BlockSpec(memory_space=pltpu.SMEM if i < tables else pltpu.VMEM)
        for i in range(len(operands))
    ]
    return pl.pallas_call(
        kernel,
        out_shape=out_shapes,
        in_specs=specs,
        out_specs=[pl.BlockSpec(memory_space=pltpu.VMEM)] * len(out_shapes),
        scratch_shapes=scratch,
        compiler_params=pltpu.CompilerParams(vmem_limit_bytes=VMEM_LIMIT),
        cost_estimate=pl.CostEstimate(flops=flops, bytes_accessed=moved, transcendentals=0),
    )(*operands)


def body(vector, right_sector, left_env, right_env, term_ops, term_left, group_right):
    terms = lax.axis_size("term")
    secs = lax.axis_size("sec")
    per_device, per_left, wide, row_width = vector.shape
    phys = row_width // wide
    lane = 2 * wide
    blocks = per_device * per_left
    slots = blocks // terms
    pairs = slots // 2
    span = secs // terms
    each = blocks // secs
    env_width = left_env.shape[1]
    depth = -(-env_width // 16) * 16
    local = group_right.shape[0]
    groups = local * terms
    slab = wide // terms
    d = lax.axis_index("sec")
    me = lax.axis_index("term")
    both_axes = ("sec", "term")
    vec = vector.reshape(blocks, wide, row_width)

    lines = terms // 2

    def flip(t, a):
        return (2 * a + (t + a) % 2) * lines + t // 2

    flat = right_sector.reshape(blocks)
    dest = flat // per_device
    before = jnp.arange(blocks)[None, :] < jnp.arange(blocks)[:, None]
    rank = jnp.sum((dest[None, :] == dest[:, None]) & before, axis=1)
    flips = dest ^ d
    a = flips // lines // 2
    t = flips % lines * 2 + (flips // lines + a) % 2
    place = t * slots + a * each + rank
    hit = place[None, :] == jnp.arange(blocks)[:, None]
    order = jnp.sum(jnp.where(hit, jnp.arange(blocks)[None, :], 0), axis=1)
    by_place = jnp.sum(jnp.where(hit, (flat % per_device)[None, :], 0), axis=1)
    own = lax.dynamic_slice(order, (me * slots,), (slots,)).astype(jnp.int32)
    wanted = lax.dynamic_slice(by_place, (me * slots,), (slots,)).astype(jnp.int32)
    table = jnp.concatenate([order.astype(jnp.int32), me.reshape(1)])

    swaps = [
        [(e * terms + t, (e ^ flip(t, a)) * terms + t) for e in range(secs) for t in range(terms)]
        for a in range(span)
    ]
    asked = [
        lax.ppermute(wanted[a * each : (a + 1) * each], both_axes, swaps[a]) for a in range(span)
    ]

    onehot = (term_left[:, :, None] == jnp.arange(depth)).astype(BF)
    operator = jnp.einsum(
        "gtys,gtw->gysw", term_ops, onehot, preferred_element_type=F32
    ).reshape(local * phys, phys * depth)
    names = jnp.pad(
        group_right.astype(F32)[None, :], ((0, 15), (0, phys * depth - local))
    )
    packed = jnp.concatenate([operator, names], axis=0).astype(BF)

    def shift(value, k):
        return lax.ppermute(value, "term", [(t, t ^ k) for t in range(terms)])

    parts = [packed] + [shift(packed, k) for k in range(1, terms)]
    known = jnp.concatenate([p[local * phys, :local] for p in parts]).astype(jnp.int32)
    asked = jnp.concatenate(asked)

    right_shape = jax.ShapeDtypeStruct((each, wide, groups * wide), BF)
    chosen = call(
        functools.partial(select_kernel, wide, [(i // each, i % each) for i in range(slots)]),
        2,
        (known, asked, right_env),
        [right_shape] * span,
        [
            pltpu.VMEM((-(-env_width // 8) * 8 * (wide // 2), lane), F32),
            pltpu.VMEM((wide, lane), F32),
        ],
        0,
        slots * env_width * wide * wide * 2,
    )
    rights = [lax.ppermute(chosen[a], both_axes, swaps[a]) for a in range(span)]
    left_env, _ = lax.optimization_barrier((left_env, chosen))

    rows = wide * depth
    left_flops = 2 * rows * 4 * wide * phys * lane
    mix_flops = 2 * groups * phys * phys * depth * wide * lane
    right_flops = 2 * wide * phys * groups * lane * lane

    def stacked(*shape):
        return jax.ShapeDtypeStruct(shape, BF)

    mixed_shape = (wide * phys, groups * lane)
    rhs_scratch = pltpu.VMEM((4 * wide, phys * lane), BF)
    con_scratch = pltpu.VMEM((rows, phys * lane), BF)
    acc_scratch = pltpu.VMEM((wide * phys, lane), F32)
    mixes, boths, lefts, amat = call(
        functools.partial(left_kernel, per_left, wide, phys),
        1,
        (own, left_env, vec, *parts),
        [
            stacked(pairs, *mixed_shape),
            stacked(pairs, wide, phys * lane),
            stacked(pairs, rows, 4 * wide),
            stacked(groups * phys, phys * depth),
        ],
        [rhs_scratch, con_scratch],
        pairs * (left_flops + mix_flops),
        pairs * wide * phys * groups * lane * 2,
    )

    where = me.reshape(1).astype(jnp.int32)
    kinds = [[((2 * pi + b) // each, (2 * pi + b) % each) for b in range(2)] for pi in range(pairs)]
    images, line, rmats, *pieces = call(
        functools.partial(right_kernel, terms, kinds, wide, phys),
        1,
        (where, mixes, boths, *rights),
        [
            stacked(pairs, wide, phys * lane),
            jax.ShapeDtypeStruct((secs * terms, 1, lane), F32),
            stacked(pairs, lane, groups * lane),
        ]
        + [stacked(pairs, slab, phys * lane)] * terms,
        [pltpu.VMEM((pairs, wide * phys, lane), F32)],
        pairs * right_flops,
        pairs * wide * phys * groups * lane * 2,
    )

    everyone = lax.all_to_all(line, both_axes, 0, 0, tiled=True).reshape(-1, lane)

    second_pieces = []
    for pi in range(pairs):
        carried = pieces if pi == 0 else []
        outs = call(
            functools.partial(second_kernel, terms, pi, wide, phys),
            1,
            (where, everyone, boths, images, lefts, amat, rmats, *carried),
            [stacked(pairs + 1 if carried else 1, slab, phys * lane)] * terms,
            [rhs_scratch, con_scratch, pltpu.VMEM(mixed_shape, BF), acc_scratch],
            left_flops + mix_flops + right_flops,
            4 * wide * phys * lane * 2,
        )
        second_pieces.append([outs[0]] + [shift(outs[k], k) for k in range(1, terms)])

    out_shape = jax.ShapeDtypeStruct((blocks, slab, row_width), BF)
    first_image, next_rows = call(
        functools.partial(place_kernel, terms, wide, phys, pairs, True),
        1,
        (table, everyone, vec, *second_pieces[0]),
        [out_shape] * 2,
        [],
        0,
        blocks * slab * row_width * 8,
    )
    (second_image,) = call(
        functools.partial(place_kernel, terms, wide, phys, pairs, False),
        1,
        (table, *(piece for one_pair in second_pieces for piece in one_pair)),
        [out_shape],
        [],
        0,
        blocks * slab * row_width * 4,
    )
    shape = (per_device, per_left, slab, row_width)
    return (first_image.reshape(shape), next_rows.reshape(shape), second_image.reshape(shape))


def solution(mesh):
    in_specs = (
        P("sec", None, None, None),
        P("sec", None),
        P("sec", None, None),
        P("sec", None, None),
        P("term", None, None, None),
        P("term", None),
        P("term"),
    )
    out_specs = (
        P("sec", None, "term", None),
        P("sec", None, "term", None),
        P("sec", None, "term", None),
    )
    return jax.shard_map(body, mesh=mesh, in_specs=in_specs, out_specs=out_specs, check_vma=False)
```

```python
import functools

import jax
import jax.numpy as jnp
from jax import lax
from jax.experimental import pallas as pl
from jax.experimental.pallas import tpu as pltpu
from jax.sharding import PartitionSpec as P

BF = jnp.bfloat16
F32 = jnp.float32
SUMS = 5
VMEM_LIMIT = 16 * 1024 * 1024


def low_half(shape):
    return lax.broadcasted_iota(jnp.int32, shape, len(shape) - 1) < shape[-1] // 2


def swap(tile):
    return pltpu.roll(tile, tile.shape[-1] // 2, 1)


def two_in_lanes(first, second):
    low = low_half(first.shape)
    return jnp.where(low, first, swap(second)), jnp.where(low, swap(first), second)


def fill_left(lhs, left_refs, wide):
    env_width = left_refs[0].shape[0]
    lane = 2 * wide
    depth = -(-env_width // 16) * 16
    lhs[...] = jnp.zeros_like(lhs)
    low = low_half((env_width, lane))
    for pair in range(wide // 2):
        for b, ref in enumerate(left_refs):
            tile = ref[:, pair * lane : (pair + 1) * lane].astype(F32)
            base = 2 * pair * depth
            cols = slice(b * lane, (b + 1) * lane)
            lhs[base : base + env_width, cols] = jnp.where(low, tile, 0.0).astype(BF)
            lhs[base + depth : base + depth + env_width, cols] = jnp.where(low, 0.0, tile).astype(BF)


def put_source(rhs, s, tile):
    rows, lane = tile.shape
    low = low_half(tile.shape)
    kept = (jnp.where(low, tile, 0.0).astype(BF), jnp.where(low, 0.0, tile).astype(BF))
    for b in range(2):
        for copy in range(2):
            base = (2 * b + copy) * rows
            rhs[base : base + rows, s * lane : (s + 1) * lane] = kept[b]


def contract_left(lhs, first, rhs, con):
    step, chunk = 256, min(512, con.shape[0])
    for n in range(rhs.shape[1] // step):
        cols = slice(n * step, (n + 1) * step)

        def one(i, carry):
            rows = pl.ds(pl.multiple_of(i * chunk, chunk), chunk)
            source = pl.ds(pl.multiple_of(first + i * chunk, chunk), chunk)
            con[rows, cols] = jnp.dot(
                lhs[source, :], rhs[:, cols], preferred_element_type=F32
            ).astype(BF)
            return carry

        lax.fori_loop(0, con.shape[0] // chunk, one, 0, unroll=True)


def mix(amat, con, mixed, phys, lane):
    depth = amat.shape[1] // phys
    groups = amat.shape[0] // phys
    pairs = con.shape[0] // depth // 2

    def one(pair, carry):
        halves = []
        for parity in range(2):
            rows = pl.ds(pl.multiple_of((2 * pair + parity) * depth, depth), depth)
            halves.append(
                jnp.concatenate(
                    [con[rows, s * lane : (s + 1) * lane] for s in range(phys)], axis=0
                )
            )
        out = jnp.dot(
            amat[...], jnp.concatenate(halves, axis=1), preferred_element_type=F32
        ).astype(BF)
        for parity in range(2):
            rows = pl.ds(pl.multiple_of((2 * pair + parity) * phys, phys), phys)
            for g in range(groups):
                mixed[rows, g * lane : (g + 1) * lane] = out[
                    g * phys : (g + 1) * phys, parity * lane : (parity + 1) * lane
                ]
        return carry

    lax.fori_loop(0, pairs, one, 0, unroll=True)


def fill_right(rmat, right_tiles, lane):
    for b, get in enumerate(right_tiles):
        wide = lane // 2
        rows = slice(b * wide, (b + 1) * wide)
        low = low_half((wide, lane))
        for pair in range(rmat.shape[1] // (2 * lane)):
            tile = get(pair).astype(F32)
            turned = swap(tile)
            if b == 0:
                first, second = jnp.where(low, tile, 0.0), jnp.where(low, turned, 0.0)
            else:
                first, second = jnp.where(low, 0.0, turned), jnp.where(low, 0.0, tile)
            rmat[rows, 2 * pair * lane : (2 * pair + 1) * lane] = first.astype(BF)
            rmat[rows, (2 * pair + 1) * lane : (2 * pair + 2) * lane] = second.astype(BF)


def contract_right(mixed, rmat, acc, chunk=256):
    for i in range(mixed.shape[0] // chunk):
        rows = slice(i * chunk, (i + 1) * chunk)
        acc[rows, :] = lax.dot_general(
            mixed[rows, :], rmat[...], (((1,), (1,)), ((), ())), preferred_element_type=F32
        )


def copy_operator(amat, parts):
    rows = amat.shape[0] // len(parts)
    for k, part in enumerate(parts):
        amat[k * rows : (k + 1) * rows, :] = part[:rows, :]


def left_kernel(per_left, wide, phys, own, left_env, vec, *refs):
    parts = refs[:-6]
    mixes, boths, lefts, amat, rhs, con = refs[-6:]
    lane = 2 * wide
    copy_operator(amat, parts)

    def one(pi, carry):
        first, second = own[2 * pi], own[2 * pi + 1]
        both, lhs = boths.at[pi], lefts.at[pi]
        fill_left(lhs, [left_env.at[lax.div(n, per_left)] for n in (first, second)], wide)
        for pair in range(phys // 2):
            cols = slice(pair * lane, (pair + 1) * lane)
            tiles = two_in_lanes(vec[first, :, cols].astype(F32), vec[second, :, cols].astype(F32))
            for half, tile in enumerate(tiles):
                s = 2 * pair + half
                both[:, s * lane : (s + 1) * lane] = tile.astype(BF)
                put_source(rhs, s, tile)
        contract_left(lhs, 0, rhs, con)
        mix(amat, con, mixes.at[pi], phys, lane)
        return carry

    lax.fori_loop(0, boths.shape[0], one, 0)


def quarter_of(place, k, rows):
    return pl.multiple_of(lax.bitwise_xor(place[0], k) * rows, rows)


def right_kernel(terms, kinds, wide, phys, place, mixes, boths, *refs):
    pairs = len(kinds)
    count = len({at for pair in kinds for at, _ in pair})
    rights, refs = refs[:count], refs[count:]
    images, line, rmats = refs[:3]
    outs, accs = refs[3 : 3 + terms], refs[3 + terms]
    lane = 2 * wide
    slab = wide // terms
    at = lax.broadcasted_iota(jnp.int32, (1, lane), 1)
    row = jnp.zeros((1, lane), F32)
    for pi in range(pairs):
        both, image = boths.at[pi], images.at[pi]
        fill_right(rmats.at[pi], tiles_of(rights, kinds[pi], lane), lane)
        acc = accs.at[pi]
        contract_right(mixes.at[pi], rmats.at[pi], acc)
        norm = jnp.zeros((wide, lane), F32)
        corr = jnp.zeros((wide, lane), F32)
        for y in range(phys):
            cols = slice(y * lane, (y + 1) * lane)
            tile = acc[pl.ds(y, wide, stride=phys), :].astype(BF)
            image[:, cols] = tile
            value = tile.astype(F32)
            vec = both[:, cols].astype(F32)
            norm += vec * vec
            corr += vec * value
        norm = jnp.sum(norm, keepdims=True)
        corr = jnp.sum(corr, keepdims=True)
        ratio = jnp.where(norm > 0, corr / jnp.where(norm > 0, norm, 1.0), 0.0)
        square = jnp.zeros((wide, lane), F32)
        cross = jnp.zeros((wide, lane), F32)
        for y in range(phys):
            cols = slice(y * lane, (y + 1) * lane)
            vec = both[:, cols].astype(F32)
            rest = image[:, cols].astype(F32) - ratio * vec
            square += rest * rest
            cross += rest * vec
        square = jnp.sum(square, keepdims=True)
        cross = jnp.sum(cross, keepdims=True)
        for i, value in enumerate((norm, corr, ratio, square, cross)):
            row = jnp.where(at == SUMS * pi + i, value, row)
        for k, out in enumerate(outs):
            out[pi] = image[pl.ds(quarter_of(place, k, slab), slab), :]
    line[...] = jnp.broadcast_to(row[None], line.shape)


def tiles_of(rights, kind, lane):
    return [
        lambda pair, ref=rights[array], at=at: ref[at, :, pair * lane : (pair + 1) * lane]
        for array, at in kind
    ]


def scalars(everyone, pairs):
    def all_of(i):
        return [everyone[:, SUMS * pi + i : SUMS * pi + i + 1] for pi in range(pairs)]

    def total(columns):
        return jnp.sum(functools.reduce(jnp.add, columns), keepdims=True)

    norm_sq = total(all_of(0))
    ratio = total(all_of(1)) / norm_sq
    rests = []
    for norm, own, square, cross in zip(*(all_of(i) for i in (0, 2, 3, 4))):
        off = own - ratio
        rests.append(square + 2 * off * cross + off * off * norm)
    return ratio, jnp.sqrt(norm_sq / (total(rests) + 1e-06))


def product_rows(place, chip, lhs, rhs, amat, rmat, outs, scratch, phys):
    con, mixed, acc = scratch
    lane = acc.shape[1]
    slab = outs[0].shape[0]
    other = lax.bitwise_xor(lax.div(place[0], 2), chip)
    contract_left(lhs, other * con.shape[0], rhs, con)
    mix(amat, con, mixed, phys, lane)
    contract_right(mixed, rmat, acc)
    for k, out in enumerate(outs):
        at = lax.rem(lax.bitwise_xor(place[0], k), 2) * slab * phys
        for y in range(phys):
            out[:, y * lane : (y + 1) * lane] = acc[pl.ds(at + y, slab, stride=phys), :].astype(BF)


def far_kernel(terms, pi, phys, place, everyone, boths, images, lefts, amat, rmats, *refs):
    far = terms - 2
    carried = refs[:far] if pi == 0 else ()
    outs = refs[len(carried) : len(carried) + far]
    rhs, *scratch = refs[len(carried) + far :]
    lane = boths.shape[2] // phys
    ratio, scale = scalars(everyone, boths.shape[0])
    for s in range(phys):
        cols = slice(s * lane, (s + 1) * lane)
        rest = images[pi, :, cols].astype(F32) - ratio * boths[pi, :, cols].astype(F32)
        put_source(rhs, s, (rest * scale).astype(BF).astype(F32))
    for out, piece in zip(outs, carried):
        out[: piece.shape[0]] = piece[...]
    last = outs[0].shape[0] - 1
    for chip in range(1, terms // 2):
        both = [outs[2 * chip - 2 + k].at[last] for k in range(2)]
        product_rows(place, chip, lefts.at[pi], rhs, amat, rmats.at[pi], both, scratch, phys)


def near_kernel(pairs, phys, place, lefts, amat, rmats, *refs):
    sources, outs, scratch = refs[:pairs], refs[pairs : pairs + 2], refs[pairs + 2 :]
    for pi in range(pairs):
        both = [out.at[pi] for out in outs]
        product_rows(
            place, 0, lefts.at[pi], sources[pi], amat, rmats.at[pi], both, scratch, phys
        )


def select_kernel(wide, blocks, names, asked, right_env, *refs):
    outs = refs[:-2]
    spread, rows_out = refs[-2:]
    env_width = right_env.shape[1]
    lane = 2 * wide
    half = wide // 2
    groups = outs[0].shape[2] // wide
    for i, (out, at) in enumerate(blocks):
        env = right_env.at[asked[i]]
        for z in range(half):
            tile = env[:, z * lane : (z + 1) * lane].astype(F32)
            for top in range(0, env_width, 8):
                part = tile[top : top + 8]
                base = top * half + z * 8
                spread[base : base + part.shape[0], :] = part

        def rows_of(g):
            name = names[g]
            return spread[pl.ds((name // 8) * (8 * half) + name % 8, half, stride=8), :]

        for pair in range(groups // 2):
            even, odd = two_in_lanes(rows_of(2 * pair), rows_of(2 * pair + 1))
            rows_out[pl.ds(0, half, stride=2), :] = even
            rows_out[pl.ds(1, half, stride=2), :] = odd
            outs[out][at, :, pair * lane : (pair + 1) * lane] = rows_out[...].astype(BF)


def place_kernel(terms, wide, phys, count, follows, table, *refs):
    if follows:
        ratio, scale = scalars(refs[0], count)
        vec, refs = refs[1], refs[2:]
        out, following = refs[-2:]
    else:
        out = refs[-1]
    lane = 2 * wide
    blocks, slab, _ = out.shape
    slots = blocks // terms
    me = table[blocks]
    for k in range(terms):
        source = lax.bitwise_xor(me, k)
        for pi in range(count):
            if follows or k < 2:
                piece = refs[k].at[pi]
            elif pi == 0:
                piece = refs[k].at[count]
            else:
                piece = refs[terms + (pi - 1) * (terms - 2) + k - 2].at[0]
            first = table[source * slots + 2 * pi]
            second = table[source * slots + 2 * pi + 1]
            for pair in range(phys // 2):
                cols = slice(pair * lane, (pair + 1) * lane)
                both = two_in_lanes(
                    piece[:, 2 * pair * lane : (2 * pair + 1) * lane].astype(F32),
                    piece[:, (2 * pair + 1) * lane : (2 * pair + 2) * lane].astype(F32),
                )
                for where, value in zip((first, second), both):
                    out[where, :, cols] = value.astype(BF)
                    if follows:
                        rows = pl.ds(pl.multiple_of(me * slab, slab), slab)
                        rest = value - ratio * vec[where, rows, cols].astype(F32)
                        following[where, :, cols] = (rest * scale).astype(BF)


def call(kernel, tables, operands, out_shapes, scratch, flops, moved):
    specs = [
        pl.BlockSpec(memory_space=pltpu.SMEM if i < tables else pltpu.VMEM)
        for i in range(len(operands))
    ]
    return pl.pallas_call(
        kernel,
        out_shape=out_shapes,
        in_specs=specs,
        out_specs=[pl.BlockSpec(memory_space=pltpu.VMEM)] * len(out_shapes),
        scratch_shapes=scratch,
        compiler_params=pltpu.CompilerParams(vmem_limit_bytes=VMEM_LIMIT),
        cost_estimate=pl.CostEstimate(flops=flops // 64, bytes_accessed=moved // 64, transcendentals=0),
    )(*operands)


def body(vector, right_sector, left_env, right_env, term_ops, term_left, group_right):
    terms = lax.axis_size("term")
    secs = lax.axis_size("sec")
    per_device, per_left, wide, row_width = vector.shape
    phys = row_width // wide
    lane = 2 * wide
    blocks = per_device * per_left
    slots = blocks // terms
    pairs = slots // 2
    span = secs // terms
    each = blocks // secs
    env_width = left_env.shape[1]
    depth = -(-env_width // 16) * 16
    local = group_right.shape[0]
    groups = local * terms
    slab = wide // terms
    d = lax.axis_index("sec")
    me = lax.axis_index("term")
    both_axes = ("sec", "term")
    vec = vector.reshape(blocks, wide, row_width)

    lines = terms // 2

    def flip(t, a):
        return (2 * a + (t + a) % 2) * lines + t // 2

    flat = right_sector.reshape(blocks)
    dest = flat // per_device
    before = jnp.arange(blocks)[None, :] < jnp.arange(blocks)[:, None]
    rank = jnp.sum((dest[None, :] == dest[:, None]) & before, axis=1)
    flips = dest ^ d
    a = flips // lines // 2
    t = flips % lines * 2 + (flips // lines + a) % 2
    place = t * slots + a * each + rank
    hit = place[None, :] == jnp.arange(blocks)[:, None]
    order = jnp.sum(jnp.where(hit, jnp.arange(blocks)[None, :], 0), axis=1)
    by_place = jnp.sum(jnp.where(hit, (flat % per_device)[None, :], 0), axis=1)
    own = lax.dynamic_slice(order, (me * slots,), (slots,)).astype(jnp.int32)
    wanted = lax.dynamic_slice(by_place, (me * slots,), (slots,)).astype(jnp.int32)
    table = jnp.concatenate([order.astype(jnp.int32), me.reshape(1)])

    swaps = [
        [(e * terms + t, (e ^ flip(t, a)) * terms + t) for e in range(secs) for t in range(terms)]
        for a in range(span)
    ]
    asked = [
        lax.ppermute(wanted[a * each : (a + 1) * each], both_axes, swaps[a]) for a in range(span)
    ]

    onehot = (term_left[:, :, None] == jnp.arange(depth)).astype(BF)
    operator = jnp.einsum(
        "gtys,gtw->gysw", term_ops, onehot, preferred_element_type=F32
    ).reshape(local * phys, phys * depth)
    names = jnp.pad(
        group_right.astype(F32)[None, :], ((0, 15), (0, phys * depth - local))
    )
    packed = jnp.concatenate([operator, names], axis=0).astype(BF)

    def shift(value, k):
        return lax.ppermute(value, "term", [(t, t ^ k) for t in range(terms)])

    parts = [packed] + [shift(packed, k) for k in range(1, terms)]
    known = jnp.concatenate([p[local * phys, :local] for p in parts]).astype(jnp.int32)
    asked = jnp.concatenate(asked)

    right_shape = jax.ShapeDtypeStruct((each, wide, groups * wide), BF)
    chosen = call(
        functools.partial(select_kernel, wide, [(i // each, i % each) for i in range(slots)]),
        2,
        (known, asked, right_env),
        [right_shape] * span,
        [
            pltpu.VMEM((-(-env_width // 8) * 8 * (wide // 2), lane), F32),
            pltpu.VMEM((wide, lane), F32),
        ],
        0,
        slots * env_width * wide * wide * 2,
    )
    rights = [lax.ppermute(chosen[a], both_axes, swaps[a]) for a in range(span)]
    left_env, _ = lax.optimization_barrier((left_env, chosen))

    rows = wide * depth
    left_flops = 2 * rows * 4 * wide * phys * lane
    mix_flops = 2 * groups * phys * phys * depth * wide * lane
    right_flops = 2 * wide * phys * groups * lane * lane

    def stacked(*shape):
        return jax.ShapeDtypeStruct(shape, BF)

    mixed_shape = (wide * phys, groups * lane)
    rhs_scratch = pltpu.VMEM((4 * wide, phys * lane), BF)
    con_scratch = pltpu.VMEM((rows, phys * lane), BF)
    acc_scratch = pltpu.VMEM((wide * phys, lane), F32)
    mixes, boths, lefts, amat = call(
        functools.partial(left_kernel, per_left, wide, phys),
        1,
        (own, left_env, vec, *parts),
        [
            stacked(pairs, *mixed_shape),
            stacked(pairs, wide, phys * lane),
            stacked(pairs, rows, 4 * wide),
            stacked(groups * phys, phys * depth),
        ],
        [rhs_scratch, con_scratch],
        pairs * (left_flops + mix_flops),
        pairs * wide * phys * groups * lane * 2,
    )

    where = me.reshape(1).astype(jnp.int32)
    kinds = [[((2 * pi + b) // each, (2 * pi + b) % each) for b in range(2)] for pi in range(pairs)]
    images, line, rmats, *pieces = call(
        functools.partial(right_kernel, terms, kinds, wide, phys),
        1,
        (where, mixes, boths, *rights),
        [
            stacked(pairs, wide, phys * lane),
            jax.ShapeDtypeStruct((secs * terms, 1, lane), F32),
            stacked(pairs, lane, groups * lane),
        ]
        + [stacked(pairs, slab, phys * lane)] * terms,
        [pltpu.VMEM((pairs, wide * phys, lane), F32)],
        pairs * right_flops,
        pairs * wide * phys * groups * lane * 2,
    )

    everyone = lax.all_to_all(line, both_axes, 0, 0, tiled=True).reshape(-1, lane)
    pieces, everyone = lax.optimization_barrier((pieces, everyone))

    part_scratch = [
        pltpu.VMEM((2 * slab * depth, phys * lane), BF),
        pltpu.VMEM((2 * slab * phys, groups * lane), BF),
        pltpu.VMEM((2 * slab * phys, lane), F32),
    ]
    product_flops = left_flops + mix_flops + right_flops
    far_pieces, sources, sums = [], [], everyone
    for pi in range(pairs):
        carried = pieces[2:] if pi == 0 else []
        *outs, source = call(
            functools.partial(far_kernel, terms, pi, phys),
            1,
            (where, sums, boths, images, lefts, amat, rmats, *carried),
            [stacked(pairs + 1 if carried else 1, slab, phys * lane)] * (terms - 2)
            + [stacked(4 * wide, phys * lane)],
            part_scratch,
            product_flops * (terms - 2) // terms,
            4 * wide * phys * lane * 2,
        )
        outs, sums = lax.optimization_barrier((outs, sums))
        far_pieces.append([shift(out, k + 2) for k, out in enumerate(outs)])
        sources.append(source)
    near_pieces = call(
        functools.partial(near_kernel, pairs, phys),
        1,
        (where, lefts, amat, rmats, *sources),
        [stacked(pairs, slab, phys * lane)] * 2,
        part_scratch,
        pairs * product_flops * 2 // terms,
        4 * wide * phys * lane * 2,
    )
    near_pieces = [near_pieces[0], shift(near_pieces[1], 1)]

    out_shape = jax.ShapeDtypeStruct((blocks, slab, row_width), BF)
    first_image, next_rows = call(
        functools.partial(place_kernel, terms, wide, phys, pairs, True),
        1,
        (table, everyone, vec, pieces[0], shift(pieces[1], 1), *far_pieces[0]),
        [out_shape] * 2,
        [],
        0,
        blocks * slab * row_width * 8,
    )
    (second_image,) = call(
        functools.partial(place_kernel, terms, wide, phys, pairs, False),
        1,
        (table, *near_pieces, *(piece for one_pair in far_pieces for piece in one_pair)),
        [out_shape],
        [],
        0,
        blocks * slab * row_width * 4,
    )
    shape = (per_device, per_left, slab, row_width)
    return (first_image.reshape(shape), next_rows.reshape(shape), second_image.reshape(shape))


def solution(mesh):
    in_specs = (
        P("sec", None, None, None),
        P("sec", None),
        P("sec", None, None),
        P("sec", None, None),
        P("term", None, None, None),
        P("term", None),
        P("term"),
    )
    out_specs = (
        P("sec", None, "term", None),
        P("sec", None, "term", None),
        P("sec", None, "term", None),
    )
    return jax.shard_map(body, mesh=mesh, in_specs=in_specs, out_specs=out_specs, check_vma=False)
```

```python
import functools

import jax
import jax.numpy as jnp
from jax import lax
from jax.experimental import pallas as pl
from jax.experimental.pallas import tpu as pltpu
from jax.sharding import PartitionSpec as P

BF = jnp.bfloat16
F32 = jnp.float32
SUMS = 5
VMEM_LIMIT = 16 * 1024 * 1024


def low_half(shape):
    return lax.broadcasted_iota(jnp.int32, shape, len(shape) - 1) < shape[-1] // 2


def swap(tile):
    return pltpu.roll(tile, tile.shape[-1] // 2, 1)


def two_in_lanes(first, second):
    low = low_half(first.shape)
    return jnp.where(low, first, swap(second)), jnp.where(low, swap(first), second)


def fill_left(lhs, left_refs, wide):
    env_width = left_refs[0].shape[0]
    lane = 2 * wide
    depth = -(-env_width // 16) * 16
    lhs[...] = jnp.zeros_like(lhs)
    low = low_half((env_width, lane))
    for pair in range(wide // 2):
        for b, ref in enumerate(left_refs):
            tile = ref[:, pair * lane : (pair + 1) * lane].astype(F32)
            base = 2 * pair * depth
            cols = slice(b * lane, (b + 1) * lane)
            lhs[base : base + env_width, cols] = jnp.where(low, tile, 0.0).astype(BF)
            lhs[base + depth : base + depth + env_width, cols] = jnp.where(low, 0.0, tile).astype(BF)


def put_source(rhs, s, tile):
    rows, lane = tile.shape
    low = low_half(tile.shape)
    kept = (jnp.where(low, tile, 0.0).astype(BF), jnp.where(low, 0.0, tile).astype(BF))
    for b in range(2):
        for copy in range(2):
            base = (2 * b + copy) * rows
            rhs[base : base + rows, s * lane : (s + 1) * lane] = kept[b]


def contract_left(lhs, first, rhs, con):
    step, chunk = 256, min(512, con.shape[0])
    for n in range(rhs.shape[1] // step):
        cols = slice(n * step, (n + 1) * step)

        def one(i, carry):
            rows = pl.ds(pl.multiple_of(i * chunk, chunk), chunk)
            source = pl.ds(pl.multiple_of(first + i * chunk, chunk), chunk)
            con[rows, cols] = jnp.dot(
                lhs[source, :], rhs[:, cols], preferred_element_type=F32
            ).astype(BF)
            return carry

        lax.fori_loop(0, con.shape[0] // chunk, one, 0, unroll=True)


def mix(amat, con, mixed, phys, lane):
    depth = amat.shape[1] // phys
    groups = amat.shape[0] // phys
    pairs = con.shape[0] // depth // 2

    def one(pair, carry):
        halves = []
        for parity in range(2):
            rows = pl.ds(pl.multiple_of((2 * pair + parity) * depth, depth), depth)
            halves.append(
                jnp.concatenate(
                    [con[rows, s * lane : (s + 1) * lane] for s in range(phys)], axis=0
                )
            )
        out = jnp.dot(
            amat[...], jnp.concatenate(halves, axis=1), preferred_element_type=F32
        ).astype(BF)
        for parity in range(2):
            rows = pl.ds(pl.multiple_of((2 * pair + parity) * phys, phys), phys)
            for g in range(groups):
                mixed[rows, g * lane : (g + 1) * lane] = out[
                    g * phys : (g + 1) * phys, parity * lane : (parity + 1) * lane
                ]
        return carry

    lax.fori_loop(0, pairs, one, 0, unroll=True)


def fill_right(rmat, right_tiles, lane):
    for b, get in enumerate(right_tiles):
        wide = lane // 2
        rows = slice(b * wide, (b + 1) * wide)
        low = low_half((wide, lane))
        for pair in range(rmat.shape[1] // (2 * lane)):
            tile = get(pair).astype(F32)
            turned = swap(tile)
            if b == 0:
                first, second = jnp.where(low, tile, 0.0), jnp.where(low, turned, 0.0)
            else:
                first, second = jnp.where(low, 0.0, turned), jnp.where(low, 0.0, tile)
            rmat[rows, 2 * pair * lane : (2 * pair + 1) * lane] = first.astype(BF)
            rmat[rows, (2 * pair + 1) * lane : (2 * pair + 2) * lane] = second.astype(BF)


def contract_right(mixed, rmat, acc, chunk=256):
    for i in range(mixed.shape[0] // chunk):
        rows = slice(i * chunk, (i + 1) * chunk)
        acc[rows, :] = lax.dot_general(
            mixed[rows, :], rmat[...], (((1,), (1,)), ((), ())), preferred_element_type=F32
        )


def copy_operator(amat, parts):
    rows = amat.shape[0] // len(parts)
    for k, part in enumerate(parts):
        amat[k * rows : (k + 1) * rows, :] = part[:rows, :]


def left_kernel(per_left, wide, phys, own, left_env, vec, *refs):
    parts = refs[:-6]
    mixes, boths, lefts, amat, rhs, con = refs[-6:]
    lane = 2 * wide
    copy_operator(amat, parts)

    def one(pi, carry):
        first, second = own[2 * pi], own[2 * pi + 1]
        both, lhs = boths.at[pi], lefts.at[pi]
        fill_left(lhs, [left_env.at[lax.div(n, per_left)] for n in (first, second)], wide)
        for pair in range(phys // 2):
            cols = slice(pair * lane, (pair + 1) * lane)
            tiles = two_in_lanes(vec[first, :, cols].astype(F32), vec[second, :, cols].astype(F32))
            for half, tile in enumerate(tiles):
                s = 2 * pair + half
                both[:, s * lane : (s + 1) * lane] = tile.astype(BF)
                put_source(rhs, s, tile)
        contract_left(lhs, 0, rhs, con)
        mix(amat, con, mixes.at[pi], phys, lane)
        return carry

    lax.fori_loop(0, boths.shape[0], one, 0)


def quarter_of(place, k, rows):
    return pl.multiple_of(lax.bitwise_xor(place[0], k) * rows, rows)


def right_kernel(terms, kinds, wide, phys, place, mixes, boths, *refs):
    pairs = len(kinds)
    count = len({at for pair in kinds for at, _ in pair})
    rights, refs = refs[:count], refs[count:]
    images, line, rmats = refs[:3]
    outs, accs = refs[3 : 3 + terms], refs[3 + terms]
    lane = 2 * wide
    slab = wide // terms
    at = lax.broadcasted_iota(jnp.int32, (1, lane), 1)
    row = jnp.zeros((1, lane), F32)
    for pi in range(pairs):
        both, image = boths.at[pi], images.at[pi]
        fill_right(rmats.at[pi], tiles_of(rights, kinds[pi], lane), lane)
        acc = accs.at[pi]
        contract_right(mixes.at[pi], rmats.at[pi], acc)
        norm = jnp.zeros((wide, lane), F32)
        corr = jnp.zeros((wide, lane), F32)
        for y in range(phys):
            cols = slice(y * lane, (y + 1) * lane)
            tile = acc[pl.ds(y, wide, stride=phys), :].astype(BF)
            image[:, cols] = tile
            value = tile.astype(F32)
            vec = both[:, cols].astype(F32)
            norm += vec * vec
            corr += vec * value
        norm = jnp.sum(norm, keepdims=True)
        corr = jnp.sum(corr, keepdims=True)
        ratio = jnp.where(norm > 0, corr / jnp.where(norm > 0, norm, 1.0), 0.0)
        square = jnp.zeros((wide, lane), F32)
        cross = jnp.zeros((wide, lane), F32)
        for y in range(phys):
            cols = slice(y * lane, (y + 1) * lane)
            vec = both[:, cols].astype(F32)
            rest = image[:, cols].astype(F32) - ratio * vec
            square += rest * rest
            cross += rest * vec
        square = jnp.sum(square, keepdims=True)
        cross = jnp.sum(cross, keepdims=True)
        for i, value in enumerate((norm, corr, ratio, square, cross)):
            row = jnp.where(at == SUMS * pi + i, value, row)
        for k, out in enumerate(outs):
            out[pi] = image[pl.ds(quarter_of(place, k, slab), slab), :]
    line[...] = jnp.broadcast_to(row[None], line.shape)


def tiles_of(rights, kind, lane):
    return [
        lambda pair, ref=rights[array], at=at: ref[at, :, pair * lane : (pair + 1) * lane]
        for array, at in kind
    ]


def scalars(everyone, pairs):
    def all_of(i):
        return [everyone[:, SUMS * pi + i : SUMS * pi + i + 1] for pi in range(pairs)]

    def total(columns):
        return jnp.sum(functools.reduce(jnp.add, columns), keepdims=True)

    norm_sq = total(all_of(0))
    ratio = total(all_of(1)) / norm_sq
    rests = []
    for norm, own, square, cross in zip(*(all_of(i) for i in (0, 2, 3, 4))):
        off = own - ratio
        rests.append(square + 2 * off * cross + off * off * norm)
    return ratio, jnp.sqrt(norm_sq / (total(rests) + 1e-06))


def product_rows(place, chip, lhs, rhs, amat, rmat, outs, scratch, phys):
    con, mixed, acc = scratch
    lane = acc.shape[1]
    slab = outs[0].shape[0]
    other = lax.bitwise_xor(lax.div(place[0], 2), chip)
    contract_left(lhs, other * con.shape[0], rhs, con)
    mix(amat, con, mixed, phys, lane)
    contract_right(mixed, rmat, acc)
    for k, out in enumerate(outs):
        at = lax.rem(lax.bitwise_xor(place[0], k), 2) * slab * phys
        for y in range(phys):
            out[:, y * lane : (y + 1) * lane] = acc[pl.ds(at + y, slab, stride=phys), :].astype(BF)


def far_kernel(terms, pi, phys, place, everyone, boths, images, lefts, amat, rmats, *refs):
    far = terms - 2
    carried = refs[:far] if pi == 0 else ()
    outs = refs[len(carried) : len(carried) + far]
    rhs, *scratch = refs[len(carried) + far :]
    lane = boths.shape[2] // phys
    ratio, scale = scalars(everyone, boths.shape[0])
    for s in range(phys):
        cols = slice(s * lane, (s + 1) * lane)
        rest = images[pi, :, cols].astype(F32) - ratio * boths[pi, :, cols].astype(F32)
        put_source(rhs, s, (rest * scale).astype(BF).astype(F32))
    for out, piece in zip(outs, carried):
        out[: piece.shape[0]] = piece[...]
    last = outs[0].shape[0] - 1
    for chip in range(1, terms // 2):
        both = [outs[2 * chip - 2 + k].at[last] for k in range(2)]
        product_rows(place, chip, lefts.at[pi], rhs, amat, rmats.at[pi], both, scratch, phys)


def near_kernel(pairs, phys, place, lefts, amat, rmats, *refs):
    sources, outs, scratch = refs[:pairs], refs[pairs : 2 * pairs + 1], refs[2 * pairs + 1 :]
    for pi in range(pairs):
        both = [outs[0].at[pi], outs[1 + pi].at[0]]
        product_rows(
            place, 0, lefts.at[pi], sources[pi], amat, rmats.at[pi], both, scratch, phys
        )


def select_kernel(wide, blocks, names, asked, right_env, *refs):
    outs = refs[:-2]
    spread, rows_out = refs[-2:]
    env_width = right_env.shape[1]
    lane = 2 * wide
    half = wide // 2
    groups = outs[0].shape[2] // wide
    for i, (out, at) in enumerate(blocks):
        env = right_env.at[asked[i]]
        for z in range(half):
            tile = env[:, z * lane : (z + 1) * lane].astype(F32)
            for top in range(0, env_width, 8):
                part = tile[top : top + 8]
                base = top * half + z * 8
                spread[base : base + part.shape[0], :] = part

        def rows_of(g):
            name = names[g]
            return spread[pl.ds((name // 8) * (8 * half) + name % 8, half, stride=8), :]

        for pair in range(groups // 2):
            even, odd = two_in_lanes(rows_of(2 * pair), rows_of(2 * pair + 1))
            rows_out[pl.ds(0, half, stride=2), :] = even
            rows_out[pl.ds(1, half, stride=2), :] = odd
            outs[out][at, :, pair * lane : (pair + 1) * lane] = rows_out[...].astype(BF)


def place_kernel(terms, wide, phys, count, follows, table, *refs):
    if follows:
        ratio, scale = scalars(refs[0], count)
        vec, refs = refs[1], refs[2:]
        out, following = refs[-2:]
    else:
        out = refs[-1]
    lane = 2 * wide
    blocks, slab, _ = out.shape
    slots = blocks // terms
    me = table[blocks]
    for k in range(terms):
        source = lax.bitwise_xor(me, k)
        for pi in range(count):
            if not follows and k == 1:
                piece = refs[k][pi].at[0]
            elif follows or k < 2:
                piece = refs[k].at[pi]
            elif pi == 0:
                piece = refs[k].at[count]
            else:
                piece = refs[terms + (pi - 1) * (terms - 2) + k - 2].at[0]
            first = table[source * slots + 2 * pi]
            second = table[source * slots + 2 * pi + 1]
            for pair in range(phys // 2):
                cols = slice(pair * lane, (pair + 1) * lane)
                both = two_in_lanes(
                    piece[:, 2 * pair * lane : (2 * pair + 1) * lane].astype(F32),
                    piece[:, (2 * pair + 1) * lane : (2 * pair + 2) * lane].astype(F32),
                )
                for where, value in zip((first, second), both):
                    out[where, :, cols] = value.astype(BF)
                    if follows:
                        rows = pl.ds(pl.multiple_of(me * slab, slab), slab)
                        rest = value - ratio * vec[where, rows, cols].astype(F32)
                        following[where, :, cols] = (rest * scale).astype(BF)


def place_all(terms, wide, phys, count, table, everyone, vec, own_first, chip_first, own, *refs):
    others, (first, following, second) = refs[:-3], refs[-3:]
    far, chip = others[:-count], others[-count:]
    ahead = (own_first, chip_first, *far[: terms - 2])
    place_kernel(terms, wide, phys, count, True, table, everyone, vec, *ahead, first, following)
    place_kernel(terms, wide, phys, count, False, table, own, chip, *far, second)


def call(kernel, tables, operands, out_shapes, scratch, flops, moved):
    specs = [
        pl.BlockSpec(memory_space=pltpu.SMEM if i < tables else pltpu.VMEM)
        for i in range(len(operands))
    ]
    return pl.pallas_call(
        kernel,
        out_shape=out_shapes,
        in_specs=specs,
        out_specs=[pl.BlockSpec(memory_space=pltpu.VMEM)] * len(out_shapes),
        scratch_shapes=scratch,
        compiler_params=pltpu.CompilerParams(vmem_limit_bytes=VMEM_LIMIT),
        cost_estimate=pl.CostEstimate(flops=flops // 64, bytes_accessed=moved // 64, transcendentals=0),
    )(*operands)


def body(vector, right_sector, left_env, right_env, term_ops, term_left, group_right):
    terms = lax.axis_size("term")
    secs = lax.axis_size("sec")
    per_device, per_left, wide, row_width = vector.shape
    phys = row_width // wide
    lane = 2 * wide
    blocks = per_device * per_left
    slots = blocks // terms
    pairs = slots // 2
    span = secs // terms
    each = blocks // secs
    env_width = left_env.shape[1]
    depth = -(-env_width // 16) * 16
    local = group_right.shape[0]
    groups = local * terms
    slab = wide // terms
    d = lax.axis_index("sec")
    me = lax.axis_index("term")
    both_axes = ("sec", "term")
    vec = vector.reshape(blocks, wide, row_width)

    lines = terms // 2

    def flip(t, a):
        return (2 * a + (t + a) % 2) * lines + t // 2

    flat = right_sector.reshape(blocks)
    dest = flat // per_device
    before = jnp.arange(blocks)[None, :] < jnp.arange(blocks)[:, None]
    rank = jnp.sum((dest[None, :] == dest[:, None]) & before, axis=1)
    flips = dest ^ d
    a = flips // lines // 2
    t = flips % lines * 2 + (flips // lines + a) % 2
    place = t * slots + a * each + rank
    hit = place[None, :] == jnp.arange(blocks)[:, None]
    order = jnp.sum(jnp.where(hit, jnp.arange(blocks)[None, :], 0), axis=1)
    by_place = jnp.sum(jnp.where(hit, (flat % per_device)[None, :], 0), axis=1)
    own = lax.dynamic_slice(order, (me * slots,), (slots,)).astype(jnp.int32)
    wanted = lax.dynamic_slice(by_place, (me * slots,), (slots,)).astype(jnp.int32)
    table = jnp.concatenate([order.astype(jnp.int32), me.reshape(1)])

    swaps = [
        [(e * terms + t, (e ^ flip(t, a)) * terms + t) for e in range(secs) for t in range(terms)]
        for a in range(span)
    ]
    asked = [
        lax.ppermute(wanted[a * each : (a + 1) * each], both_axes, swaps[a]) for a in range(span)
    ]

    onehot = (term_left[:, :, None] == jnp.arange(depth)).astype(BF)
    operator = jnp.einsum(
        "gtys,gtw->gysw", term_ops, onehot, preferred_element_type=F32
    ).reshape(local * phys, phys * depth)
    names = jnp.pad(
        group_right.astype(F32)[None, :], ((0, 15), (0, phys * depth - local))
    )
    packed = jnp.concatenate([operator, names], axis=0).astype(BF)

    def shift(value, k):
        return lax.ppermute(value, "term", [(t, t ^ k) for t in range(terms)])

    parts = [packed] + [shift(packed, k) for k in range(1, terms)]
    known = jnp.concatenate([p[local * phys, :local] for p in parts]).astype(jnp.int32)
    asked = jnp.concatenate(asked)

    right_shape = jax.ShapeDtypeStruct((each, wide, groups * wide), BF)
    chosen = call(
        functools.partial(select_kernel, wide, [(i // each, i % each) for i in range(slots)]),
        2,
        (known, asked, right_env),
        [right_shape] * span,
        [
            pltpu.VMEM((-(-env_width // 8) * 8 * (wide // 2), lane), F32),
            pltpu.VMEM((wide, lane), F32),
        ],
        0,
        slots * env_width * wide * wide * 2,
    )
    rights = [lax.ppermute(chosen[a], both_axes, swaps[a]) for a in range(span)]
    left_env, _ = lax.optimization_barrier((left_env, chosen))

    rows = wide * depth
    left_flops = 2 * rows * 4 * wide * phys * lane
    mix_flops = 2 * groups * phys * phys * depth * wide * lane
    right_flops = 2 * wide * phys * groups * lane * lane

    def stacked(*shape):
        return jax.ShapeDtypeStruct(shape, BF)

    mixed_shape = (wide * phys, groups * lane)
    rhs_scratch = pltpu.VMEM((4 * wide, phys * lane), BF)
    con_scratch = pltpu.VMEM((rows, phys * lane), BF)
    acc_scratch = pltpu.VMEM((wide * phys, lane), F32)
    mixes, boths, lefts, amat = call(
        functools.partial(left_kernel, per_left, wide, phys),
        1,
        (own, left_env, vec, *parts),
        [
            stacked(pairs, *mixed_shape),
            stacked(pairs, wide, phys * lane),
            stacked(pairs, rows, 4 * wide),
            stacked(groups * phys, phys * depth),
        ],
        [rhs_scratch, con_scratch],
        pairs * (left_flops + mix_flops),
        pairs * wide * phys * groups * lane * 2,
    )

    where = me.reshape(1).astype(jnp.int32)
    kinds = [[((2 * pi + b) // each, (2 * pi + b) % each) for b in range(2)] for pi in range(pairs)]
    images, line, rmats, *pieces = call(
        functools.partial(right_kernel, terms, kinds, wide, phys),
        1,
        (where, mixes, boths, *rights),
        [
            stacked(pairs, wide, phys * lane),
            jax.ShapeDtypeStruct((secs * terms, 1, lane), F32),
            stacked(pairs, lane, groups * lane),
        ]
        + [stacked(pairs, slab, phys * lane)] * terms,
        [pltpu.VMEM((pairs, wide * phys, lane), F32)],
        pairs * right_flops,
        pairs * wide * phys * groups * lane * 2,
    )

    everyone = lax.all_to_all(line, both_axes, 0, 0, tiled=True).reshape(-1, lane)
    pieces, everyone = lax.optimization_barrier((pieces, everyone))

    part_scratch = [
        pltpu.VMEM((2 * slab * depth, phys * lane), BF),
        pltpu.VMEM((2 * slab * phys, groups * lane), BF),
        pltpu.VMEM((2 * slab * phys, lane), F32),
    ]
    product_flops = left_flops + mix_flops + right_flops
    far_pieces, sources, sums = [], [], everyone
    for pi in range(pairs):
        carried = pieces[2:] if pi == 0 else []
        *outs, source = call(
            functools.partial(far_kernel, terms, pi, phys),
            1,
            (where, sums, boths, images, lefts, amat, rmats, *carried),
            [stacked(pairs + 1 if carried else 1, slab, phys * lane)] * (terms - 2)
            + [stacked(4 * wide, phys * lane)],
            part_scratch,
            product_flops * (terms - 2) // terms,
            4 * wide * phys * lane * 2,
        )
        outs, sums = lax.optimization_barrier((outs, sums))
        far_pieces.append([shift(out, k + 2) for k, out in enumerate(outs)])
        sources.append(source)
    near_pieces = call(
        functools.partial(near_kernel, pairs, phys),
        1,
        (where, lefts, amat, rmats, *sources),
        [stacked(pairs, slab, phys * lane)] + [stacked(1, slab, phys * lane)] * pairs,
        part_scratch,
        pairs * product_flops * 2 // terms,
        4 * wide * phys * lane * 2,
    )
    near_pieces = [near_pieces[0]] + [shift(piece, 1) for piece in near_pieces[1:]]

    out_shape = jax.ShapeDtypeStruct((blocks, slab, row_width), BF)
    far = [piece for one_pair in far_pieces for piece in one_pair]
    first_image, next_rows, second_image = call(
        functools.partial(place_all, terms, wide, phys, pairs),
        1,
        (table, everyone, vec, pieces[0], shift(pieces[1], 1), near_pieces[0], *far, *near_pieces[1:]),
        [out_shape] * 3,
        [],
        0,
        blocks * slab * row_width * 12,
    )
    shape = (per_device, per_left, slab, row_width)
    return (first_image.reshape(shape), next_rows.reshape(shape), second_image.reshape(shape))


def solution(mesh):
    in_specs = (
        P("sec", None, None, None),
        P("sec", None),
        P("sec", None, None),
        P("sec", None, None),
        P("term", None, None, None),
        P("term", None),
        P("term"),
    )
    out_specs = (
        P("sec", None, "term", None),
        P("sec", None, "term", None),
        P("sec", None, "term", None),
    )
    return jax.shard_map(body, mesh=mesh, in_specs=in_specs, out_specs=out_specs, check_vma=False)
```

```python
import functools

import jax
import jax.numpy as jnp
from jax import lax
from jax.experimental import pallas as pl
from jax.experimental.pallas import tpu as pltpu
from jax.sharding import PartitionSpec as P

BF = jnp.bfloat16
F32 = jnp.float32
SUMS = 5
VMEM_LIMIT = 16 * 1024 * 1024


def low_half(shape):
    return lax.broadcasted_iota(jnp.int32, shape, len(shape) - 1) < shape[-1] // 2


def swap(tile):
    return pltpu.roll(tile, tile.shape[-1] // 2, 1)


def two_in_lanes(first, second):
    low = low_half(first.shape)
    return jnp.where(low, first, swap(second)), jnp.where(low, swap(first), second)


def fill_left(lhs, left_refs, wide):
    env_width = left_refs[0].shape[0]
    lane = 2 * wide
    depth = -(-env_width // 16) * 16
    lhs[...] = jnp.zeros_like(lhs)
    low = low_half((env_width, lane))
    for pair in range(wide // 2):
        for b, ref in enumerate(left_refs):
            tile = ref[:, pair * lane : (pair + 1) * lane].astype(F32)
            base = 2 * pair * depth
            cols = slice(b * lane, (b + 1) * lane)
            lhs[base : base + env_width, cols] = jnp.where(low, tile, 0.0).astype(BF)
            lhs[base + depth : base + depth + env_width, cols] = jnp.where(low, 0.0, tile).astype(BF)


def put_source(rhs, s, tile):
    rows, lane = tile.shape
    low = low_half(tile.shape)
    kept = (jnp.where(low, tile, 0.0).astype(BF), jnp.where(low, 0.0, tile).astype(BF))
    for b in range(2):
        for copy in range(2):
            base = (2 * b + copy) * rows
            rhs[base : base + rows, s * lane : (s + 1) * lane] = kept[b]


def contract_left(lhs, first, rhs, con):
    step, chunk = 256, min(512, con.shape[0])
    for n in range(rhs.shape[1] // step):
        cols = slice(n * step, (n + 1) * step)

        def one(i, carry):
            rows = pl.ds(pl.multiple_of(i * chunk, chunk), chunk)
            source = pl.ds(pl.multiple_of(first + i * chunk, chunk), chunk)
            con[rows, cols] = jnp.dot(
                lhs[source, :], rhs[:, cols], preferred_element_type=F32
            ).astype(BF)
            return carry

        lax.fori_loop(0, con.shape[0] // chunk, one, 0, unroll=True)


def mix(amat, con, mixed, phys, lane):
    depth = amat.shape[1] // phys
    groups = amat.shape[0] // phys
    pairs = con.shape[0] // depth // 2

    def one(pair, carry):
        halves = []
        for parity in range(2):
            rows = pl.ds(pl.multiple_of((2 * pair + parity) * depth, depth), depth)
            halves.append(
                jnp.concatenate(
                    [con[rows, s * lane : (s + 1) * lane] for s in range(phys)], axis=0
                )
            )
        out = jnp.dot(
            amat[...], jnp.concatenate(halves, axis=1), preferred_element_type=F32
        ).astype(BF)
        for parity in range(2):
            rows = pl.ds(pl.multiple_of((2 * pair + parity) * phys, phys), phys)
            for g in range(groups):
                mixed[rows, g * lane : (g + 1) * lane] = out[
                    g * phys : (g + 1) * phys, parity * lane : (parity + 1) * lane
                ]
        return carry

    lax.fori_loop(0, pairs, one, 0, unroll=True)


def fill_right(rmat, right_tiles, lane):
    for b, get in enumerate(right_tiles):
        wide = lane // 2
        rows = slice(b * wide, (b + 1) * wide)
        low = low_half((wide, lane))
        for pair in range(rmat.shape[1] // (2 * lane)):
            tile = get(pair).astype(F32)
            turned = swap(tile)
            if b == 0:
                first, second = jnp.where(low, tile, 0.0), jnp.where(low, turned, 0.0)
            else:
                first, second = jnp.where(low, 0.0, turned), jnp.where(low, 0.0, tile)
            rmat[rows, 2 * pair * lane : (2 * pair + 1) * lane] = first.astype(BF)
            rmat[rows, (2 * pair + 1) * lane : (2 * pair + 2) * lane] = second.astype(BF)


def contract_right(mixed, rmat, acc, chunk=256):
    for i in range(mixed.shape[0] // chunk):
        rows = slice(i * chunk, (i + 1) * chunk)
        acc[rows, :] = lax.dot_general(
            mixed[rows, :], rmat[...], (((1,), (1,)), ((), ())), preferred_element_type=F32
        )


def copy_operator(amat, parts):
    rows = amat.shape[0] // len(parts)
    for k, part in enumerate(parts):
        amat[k * rows : (k + 1) * rows, :] = part[:rows, :]


def left_kernel(per_left, wide, phys, own, left_env, vec, *refs):
    parts = refs[:-6]
    mixes, boths, lefts, amat, sources, con = refs[-6:]
    lane = 2 * wide
    copy_operator(amat, parts)

    pairs = boths.shape[0]
    for pi in range(pairs):
        first, second = own[2 * pi], own[2 * pi + 1]
        both, lhs, rhs = boths.at[pi], lefts.at[pi], sources.at[pi]
        fill_left(lhs, [left_env.at[lax.div(n, per_left)] for n in (first, second)], wide)
        for pair in range(phys // 2):
            cols = slice(pair * lane, (pair + 1) * lane)
            tiles = two_in_lanes(vec[first, :, cols].astype(F32), vec[second, :, cols].astype(F32))
            for half, tile in enumerate(tiles):
                s = 2 * pair + half
                both[:, s * lane : (s + 1) * lane] = tile.astype(BF)
                put_source(rhs, s, tile)
    for pi in range(pairs):
        contract_left(lefts.at[pi], 0, sources.at[pi], con)
        mix(amat, con, mixes.at[pi], phys, lane)


def quarter_of(place, k, rows):
    return pl.multiple_of(lax.bitwise_xor(place[0], k) * rows, rows)


def right_kernel(terms, kinds, wide, phys, place, mixes, boths, *refs):
    pairs = len(kinds)
    count = len({at for pair in kinds for at, _ in pair})
    rights, refs = refs[:count], refs[count:]
    images, line, rmats = refs[:3]
    outs, accs = refs[3 : 3 + terms], refs[3 + terms]
    lane = 2 * wide
    slab = wide // terms
    at = lax.broadcasted_iota(jnp.int32, (1, lane), 1)
    row = jnp.zeros((1, lane), F32)
    for pi in range(pairs):
        both, image = boths.at[pi], images.at[pi]
        fill_right(rmats.at[pi], tiles_of(rights, kinds[pi], lane), lane)
        acc = accs.at[pi]
        contract_right(mixes.at[pi], rmats.at[pi], acc)
        norm = jnp.zeros((wide, lane), F32)
        corr = jnp.zeros((wide, lane), F32)
        for y in range(phys):
            cols = slice(y * lane, (y + 1) * lane)
            tile = acc[pl.ds(y, wide, stride=phys), :].astype(BF)
            image[:, cols] = tile
            value = tile.astype(F32)
            vec = both[:, cols].astype(F32)
            norm += vec * vec
            corr += vec * value
        norm = jnp.sum(norm, keepdims=True)
        corr = jnp.sum(corr, keepdims=True)
        ratio = jnp.where(norm > 0, corr / jnp.where(norm > 0, norm, 1.0), 0.0)
        square = jnp.zeros((wide, lane), F32)
        cross = jnp.zeros((wide, lane), F32)
        for y in range(phys):
            cols = slice(y * lane, (y + 1) * lane)
            vec = both[:, cols].astype(F32)
            rest = image[:, cols].astype(F32) - ratio * vec
            square += rest * rest
            cross += rest * vec
        square = jnp.sum(square, keepdims=True)
        cross = jnp.sum(cross, keepdims=True)
        for i, value in enumerate((norm, corr, ratio, square, cross)):
            row = jnp.where(at == SUMS * pi + i, value, row)
        for k, out in enumerate(outs):
            out[pi] = image[pl.ds(quarter_of(place, k, slab), slab), :]
    line[...] = jnp.broadcast_to(row[None], line.shape)


def tiles_of(rights, kind, lane):
    return [
        lambda pair, ref=rights[array], at=at: ref[at, :, pair * lane : (pair + 1) * lane]
        for array, at in kind
    ]


def scalars(everyone, pairs):
    def all_of(i):
        return [everyone[:, SUMS * pi + i : SUMS * pi + i + 1] for pi in range(pairs)]

    def total(columns):
        return jnp.sum(functools.reduce(jnp.add, columns), keepdims=True)

    norm_sq = total(all_of(0))
    ratio = total(all_of(1)) / norm_sq
    rests = []
    for norm, own, square, cross in zip(*(all_of(i) for i in (0, 2, 3, 4))):
        off = own - ratio
        rests.append(square + 2 * off * cross + off * off * norm)
    return ratio, jnp.sqrt(norm_sq / (total(rests) + 1e-06))


def product_rows(place, chip, lhs, rhs, amat, rmat, outs, scratch, phys):
    con, mixed, acc = scratch
    lane = acc.shape[1]
    slab = outs[0].shape[0]
    other = lax.bitwise_xor(lax.div(place[0], 2), chip)
    contract_left(lhs, other * con.shape[0], rhs, con)
    mix(amat, con, mixed, phys, lane)
    contract_right(mixed, rmat, acc)
    for k, out in enumerate(outs):
        at = lax.rem(lax.bitwise_xor(place[0], k), 2) * slab * phys
        for y in range(phys):
            out[:, y * lane : (y + 1) * lane] = acc[pl.ds(at + y, slab, stride=phys), :].astype(BF)


def far_kernel(terms, pi, phys, place, everyone, boths, images, lefts, amat, rmats, *refs):
    far = terms - 2
    carried = refs[:far] if pi == 0 else ()
    outs = refs[len(carried) : len(carried) + far]
    rhs, *scratch = refs[len(carried) + far :]
    lane = boths.shape[2] // phys
    ratio, scale = scalars(everyone, boths.shape[0])
    for s in range(phys):
        cols = slice(s * lane, (s + 1) * lane)
        rest = images[pi, :, cols].astype(F32) - ratio * boths[pi, :, cols].astype(F32)
        put_source(rhs, s, (rest * scale).astype(BF).astype(F32))
    for out, piece in zip(outs, carried):
        out[: piece.shape[0]] = piece[...]
    last = outs[0].shape[0] - 1
    for chip in range(1, terms // 2):
        both = [outs[2 * chip - 2 + k].at[last] for k in range(2)]
        product_rows(place, chip, lefts.at[pi], rhs, amat, rmats.at[pi], both, scratch, phys)


def near_kernel(pairs, phys, place, lefts, amat, rmats, *refs):
    sources, outs, scratch = refs[:pairs], refs[pairs : 2 * pairs + 1], refs[2 * pairs + 1 :]
    for pi in range(pairs):
        both = [outs[0].at[pi], outs[1 + pi].at[0]]
        product_rows(
            place, 0, lefts.at[pi], sources[pi], amat, rmats.at[pi], both, scratch, phys
        )


def select_kernel(wide, blocks, names, asked, right_env, *refs):
    outs = refs[:-2]
    spread, rows_out = refs[-2:]
    env_width = right_env.shape[1]
    lane = 2 * wide
    half = wide // 2
    groups = outs[0].shape[2] // wide
    for i, (out, at) in enumerate(blocks):
        env = right_env.at[asked[i]]
        for z in range(half):
            tile = env[:, z * lane : (z + 1) * lane].astype(F32)
            for top in range(0, env_width, 8):
                part = tile[top : top + 8]
                base = top * half + z * 8
                spread[base : base + part.shape[0], :] = part

        def rows_of(g):
            name = names[g]
            return spread[pl.ds((name // 8) * (8 * half) + name % 8, half, stride=8), :]

        for pair in range(groups // 2):
            even, odd = two_in_lanes(rows_of(2 * pair), rows_of(2 * pair + 1))
            rows_out[pl.ds(0, half, stride=2), :] = even
            rows_out[pl.ds(1, half, stride=2), :] = odd
            outs[out][at, :, pair * lane : (pair + 1) * lane] = rows_out[...].astype(BF)


def place_kernel(terms, wide, phys, count, follows, table, *refs):
    if follows:
        ratio, scale = scalars(refs[0], count)
        vec, refs = refs[1], refs[2:]
        out, following = refs[-2:]
    else:
        out = refs[-1]
    lane = 2 * wide
    blocks, slab, _ = out.shape
    slots = blocks // terms
    me = table[blocks]
    for k in range(terms):
        source = lax.bitwise_xor(me, k)
        for pi in range(count):
            if not follows and k == 1:
                piece = refs[k][pi].at[0]
            elif follows or k < 2:
                piece = refs[k].at[pi]
            elif pi == 0:
                piece = refs[k].at[count]
            else:
                piece = refs[terms + (pi - 1) * (terms - 2) + k - 2].at[0]
            first = table[source * slots + 2 * pi]
            second = table[source * slots + 2 * pi + 1]
            for pair in range(phys // 2):
                cols = slice(pair * lane, (pair + 1) * lane)
                both = two_in_lanes(
                    piece[:, 2 * pair * lane : (2 * pair + 1) * lane].astype(F32),
                    piece[:, (2 * pair + 1) * lane : (2 * pair + 2) * lane].astype(F32),
                )
                for where, value in zip((first, second), both):
                    out[where, :, cols] = value.astype(BF)
                    if follows:
                        rows = pl.ds(pl.multiple_of(me * slab, slab), slab)
                        rest = value - ratio * vec[where, rows, cols].astype(F32)
                        following[where, :, cols] = (rest * scale).astype(BF)


def place_all(terms, wide, phys, count, table, everyone, vec, own_first, chip_first, own, *refs):
    others, (first, following, second) = refs[:-3], refs[-3:]
    far, chip = others[:-count], others[-count:]
    ahead = (own_first, chip_first, *far[: terms - 2])
    place_kernel(terms, wide, phys, count, True, table, everyone, vec, *ahead, first, following)
    place_kernel(terms, wide, phys, count, False, table, own, chip, *far, second)


def call(kernel, tables, operands, out_shapes, scratch, flops, moved):
    specs = [
        pl.BlockSpec(memory_space=pltpu.SMEM if i < tables else pltpu.VMEM)
        for i in range(len(operands))
    ]
    return pl.pallas_call(
        kernel,
        out_shape=out_shapes,
        in_specs=specs,
        out_specs=[pl.BlockSpec(memory_space=pltpu.VMEM)] * len(out_shapes),
        scratch_shapes=scratch,
        compiler_params=pltpu.CompilerParams(vmem_limit_bytes=VMEM_LIMIT),
        cost_estimate=pl.CostEstimate(flops=flops // 64, bytes_accessed=moved // 64, transcendentals=0),
    )(*operands)


def body(vector, right_sector, left_env, right_env, term_ops, term_left, group_right):
    terms = lax.axis_size("term")
    secs = lax.axis_size("sec")
    per_device, per_left, wide, row_width = vector.shape
    phys = row_width // wide
    lane = 2 * wide
    blocks = per_device * per_left
    slots = blocks // terms
    pairs = slots // 2
    span = secs // terms
    each = blocks // secs
    env_width = left_env.shape[1]
    depth = -(-env_width // 16) * 16
    local = group_right.shape[0]
    groups = local * terms
    slab = wide // terms
    d = lax.axis_index("sec")
    me = lax.axis_index("term")
    both_axes = ("sec", "term")
    vec = vector.reshape(blocks, wide, row_width)

    lines = terms // 2

    def flip(t, a):
        return (2 * a + (t + a) % 2) * lines + t // 2

    flat = right_sector.reshape(blocks)
    dest = flat // per_device
    before = jnp.arange(blocks)[None, :] < jnp.arange(blocks)[:, None]
    rank = jnp.sum((dest[None, :] == dest[:, None]) & before, axis=1)
    flips = dest ^ d
    a = flips // lines // 2
    t = flips % lines * 2 + (flips // lines + a) % 2
    place = t * slots + a * each + rank
    hit = place[None, :] == jnp.arange(blocks)[:, None]
    order = jnp.sum(jnp.where(hit, jnp.arange(blocks)[None, :], 0), axis=1)
    by_place = jnp.sum(jnp.where(hit, (flat % per_device)[None, :], 0), axis=1)
    own = lax.dynamic_slice(order, (me * slots,), (slots,)).astype(jnp.int32)
    wanted = lax.dynamic_slice(by_place, (me * slots,), (slots,)).astype(jnp.int32)
    table = jnp.concatenate([order.astype(jnp.int32), me.reshape(1)])

    swaps = [
        [(e * terms + t, (e ^ flip(t, a)) * terms + t) for e in range(secs) for t in range(terms)]
        for a in range(span)
    ]
    asked = [
        lax.ppermute(wanted[a * each : (a + 1) * each], both_axes, swaps[a]) for a in range(span)
    ]

    onehot = (term_left[:, :, None] == jnp.arange(depth)).astype(BF)
    operator = jnp.einsum(
        "gtys,gtw->gysw", term_ops, onehot, preferred_element_type=F32
    ).reshape(local * phys, phys * depth)
    names = jnp.pad(
        group_right.astype(F32)[None, :], ((0, 15), (0, phys * depth - local))
    )
    packed = jnp.concatenate([operator, names], axis=0).astype(BF)

    def shift(value, k):
        return lax.ppermute(value, "term", [(t, t ^ k) for t in range(terms)])

    parts = [packed] + [shift(packed, k) for k in range(1, terms)]
    known = jnp.concatenate([p[local * phys, :local] for p in parts]).astype(jnp.int32)
    asked = jnp.concatenate(asked)

    right_shape = jax.ShapeDtypeStruct((each, wide, groups * wide), BF)
    chosen = call(
        functools.partial(select_kernel, wide, [(i // each, i % each) for i in range(slots)]),
        2,
        (known, asked, right_env),
        [right_shape] * span,
        [
            pltpu.VMEM((-(-env_width // 8) * 8 * (wide // 2), lane), F32),
            pltpu.VMEM((wide, lane), F32),
        ],
        0,
        slots * env_width * wide * wide * 2,
    )
    rights = [lax.ppermute(chosen[a], both_axes, swaps[a]) for a in range(span)]
    left_env, _ = lax.optimization_barrier((left_env, chosen))

    rows = wide * depth
    left_flops = 2 * rows * 4 * wide * phys * lane
    mix_flops = 2 * groups * phys * phys * depth * wide * lane
    right_flops = 2 * wide * phys * groups * lane * lane

    def stacked(*shape):
        return jax.ShapeDtypeStruct(shape, BF)

    mixed_shape = (wide * phys, groups * lane)
    rhs_scratch = pltpu.VMEM((4 * wide, phys * lane), BF)
    con_scratch = pltpu.VMEM((rows, phys * lane), BF)
    acc_scratch = pltpu.VMEM((wide * phys, lane), F32)
    mixes, boths, lefts, amat = call(
        functools.partial(left_kernel, per_left, wide, phys),
        1,
        (own, left_env, vec, *parts),
        [
            stacked(pairs, *mixed_shape),
            stacked(pairs, wide, phys * lane),
            stacked(pairs, rows, 4 * wide),
            stacked(groups * phys, phys * depth),
        ],
        [pltpu.VMEM((pairs, 4 * wide, phys * lane), BF), con_scratch],
        pairs * (left_flops + mix_flops),
        pairs * wide * phys * groups * lane * 2,
    )

    where = me.reshape(1).astype(jnp.int32)
    kinds = [[((2 * pi + b) // each, (2 * pi + b) % each) for b in range(2)] for pi in range(pairs)]
    images, line, rmats, *pieces = call(
        functools.partial(right_kernel, terms, kinds, wide, phys),
        1,
        (where, mixes, boths, *rights),
        [
            stacked(pairs, wide, phys * lane),
            jax.ShapeDtypeStruct((secs * terms, 1, lane), F32),
            stacked(pairs, lane, groups * lane),
        ]
        + [stacked(pairs, slab, phys * lane)] * terms,
        [pltpu.VMEM((pairs, wide * phys, lane), F32)],
        pairs * right_flops,
        pairs * wide * phys * groups * lane * 2,
    )

    everyone = lax.all_to_all(line, both_axes, 0, 0, tiled=True).reshape(-1, lane)
    pieces, everyone = lax.optimization_barrier((pieces, everyone))

    part_scratch = [
        pltpu.VMEM((2 * slab * depth, phys * lane), BF),
        pltpu.VMEM((2 * slab * phys, groups * lane), BF),
        pltpu.VMEM((2 * slab * phys, lane), F32),
    ]
    product_flops = left_flops + mix_flops + right_flops
    far_pieces, sources, sums = [], [], everyone
    for pi in range(pairs):
        carried = pieces[2:] if pi == 0 else []
        *outs, source = call(
            functools.partial(far_kernel, terms, pi, phys),
            1,
            (where, sums, boths, images, lefts, amat, rmats, *carried),
            [stacked(pairs + 1 if carried else 1, slab, phys * lane)] * (terms - 2)
            + [stacked(4 * wide, phys * lane)],
            part_scratch,
            product_flops * (terms - 2) // terms,
            4 * wide * phys * lane * 2,
        )
        outs, sums = lax.optimization_barrier((outs, sums))
        far_pieces.append([shift(out, k + 2) for k, out in enumerate(outs)])
        sources.append(source)
    near_pieces = call(
        functools.partial(near_kernel, pairs, phys),
        1,
        (where, lefts, amat, rmats, *sources),
        [stacked(pairs, slab, phys * lane)] + [stacked(1, slab, phys * lane)] * pairs,
        part_scratch,
        pairs * product_flops * 2 // terms,
        4 * wide * phys * lane * 2,
    )
    near_pieces = [near_pieces[0]] + [shift(piece, 1) for piece in near_pieces[1:]]

    out_shape = jax.ShapeDtypeStruct((blocks, slab, row_width), BF)
    far = [piece for one_pair in far_pieces for piece in one_pair]
    first_image, next_rows, second_image = call(
        functools.partial(place_all, terms, wide, phys, pairs),
        1,
        (table, everyone, vec, pieces[0], shift(pieces[1], 1), near_pieces[0], *far, *near_pieces[1:]),
        [out_shape] * 3,
        [],
        0,
        blocks * slab * row_width * 12,
    )
    shape = (per_device, per_left, slab, row_width)
    return (first_image.reshape(shape), next_rows.reshape(shape), second_image.reshape(shape))


def solution(mesh):
    in_specs = (
        P("sec", None, None, None),
        P("sec", None),
        P("sec", None, None),
        P("sec", None, None),
        P("term", None, None, None),
        P("term", None),
        P("term"),
    )
    out_specs = (
        P("sec", None, "term", None),
        P("sec", None, "term", None),
        P("sec", None, "term", None),
    )
    return jax.shard_map(body, mesh=mesh, in_specs=in_specs, out_specs=out_specs, check_vma=False)
```

```python
import functools

import jax
import jax.numpy as jnp
from jax import lax
from jax.experimental import pallas as pl
from jax.experimental.pallas import tpu as pltpu
from jax.sharding import PartitionSpec as P

BF = jnp.bfloat16
F32 = jnp.float32
SUMS = 5
VMEM_LIMIT = 16 * 1024 * 1024


def low_half(shape):
    return lax.broadcasted_iota(jnp.int32, shape, len(shape) - 1) < shape[-1] // 2


def swap(tile):
    return pltpu.roll(tile, tile.shape[-1] // 2, 1)


def two_in_lanes(first, second):
    low = low_half(first.shape)
    return jnp.where(low, first, swap(second)), jnp.where(low, swap(first), second)


def fill_left(lhs, left_refs, wide):
    env_width = left_refs[0].shape[0]
    lane = 2 * wide
    depth = -(-env_width // 16) * 16
    lhs[...] = jnp.zeros_like(lhs)
    low = low_half((env_width, lane))
    for pair in range(wide // 2):
        for b, ref in enumerate(left_refs):
            tile = ref[:, pair * lane : (pair + 1) * lane].astype(F32)
            base = 2 * pair * depth
            cols = slice(b * lane, (b + 1) * lane)
            lhs[base : base + env_width, cols] = jnp.where(low, tile, 0.0).astype(BF)
            lhs[base + depth : base + depth + env_width, cols] = jnp.where(low, 0.0, tile).astype(BF)


def put_source(rhs, s, tile):
    rows, lane = tile.shape
    low = low_half(tile.shape)
    kept = (jnp.where(low, tile, 0.0).astype(BF), jnp.where(low, 0.0, tile).astype(BF))
    for b in range(2):
        for copy in range(2):
            base = (2 * b + copy) * rows
            rhs[base : base + rows, s * lane : (s + 1) * lane] = kept[b]


def contract_left(lhs, first, rhs, con):
    step, chunk = 256, min(512, con.shape[0])
    for n in range(rhs.shape[1] // step):
        cols = slice(n * step, (n + 1) * step)

        def one(i, carry):
            rows = pl.ds(pl.multiple_of(i * chunk, chunk), chunk)
            source = pl.ds(pl.multiple_of(first + i * chunk, chunk), chunk)
            con[rows, cols] = jnp.dot(
                lhs[source, :], rhs[:, cols], preferred_element_type=F32
            ).astype(BF)
            return carry

        lax.fori_loop(0, con.shape[0] // chunk, one, 0, unroll=True)


def mix(amat, con, mixed, phys, lane):
    depth = amat.shape[1] // phys
    groups = amat.shape[0] // phys
    pairs = con.shape[0] // depth // 2

    def one(pair, carry):
        halves = []
        for parity in range(2):
            rows = pl.ds(pl.multiple_of((2 * pair + parity) * depth, depth), depth)
            halves.append(
                jnp.concatenate(
                    [con[rows, s * lane : (s + 1) * lane] for s in range(phys)], axis=0
                )
            )
        out = jnp.dot(
            amat[...], jnp.concatenate(halves, axis=1), preferred_element_type=F32
        ).astype(BF)
        for parity in range(2):
            rows = pl.ds(pl.multiple_of((2 * pair + parity) * phys, phys), phys)
            for g in range(groups):
                mixed[rows, g * lane : (g + 1) * lane] = out[
                    g * phys : (g + 1) * phys, parity * lane : (parity + 1) * lane
                ]
        return carry

    lax.fori_loop(0, pairs, one, 0, unroll=True)


def fill_right(rmat, right_tiles, lane):
    for b, get in enumerate(right_tiles):
        wide = lane // 2
        rows = slice(b * wide, (b + 1) * wide)
        low = low_half((wide, lane))
        for pair in range(rmat.shape[1] // (2 * lane)):
            tile = get(pair).astype(F32)
            turned = swap(tile)
            if b == 0:
                first, second = jnp.where(low, tile, 0.0), jnp.where(low, turned, 0.0)
            else:
                first, second = jnp.where(low, 0.0, turned), jnp.where(low, 0.0, tile)
            rmat[rows, 2 * pair * lane : (2 * pair + 1) * lane] = first.astype(BF)
            rmat[rows, (2 * pair + 1) * lane : (2 * pair + 2) * lane] = second.astype(BF)


def contract_right(mixed, rmat, acc, chunk=256):
    for i in range(mixed.shape[0] // chunk):
        rows = slice(i * chunk, (i + 1) * chunk)
        acc[rows, :] = lax.dot_general(
            mixed[rows, :], rmat[...], (((1,), (1,)), ((), ())), preferred_element_type=F32
        )


def copy_operator(amat, parts):
    rows = amat.shape[0] // len(parts)
    for k, part in enumerate(parts):
        amat[k * rows : (k + 1) * rows, :] = part[:rows, :]


def left_kernel(per_left, wide, phys, own, left_env, vec, *refs):
    parts = refs[:-6]
    mixes, boths, lefts, amat, sources, con = refs[-6:]
    lane = 2 * wide
    copy_operator(amat, parts)

    pairs = boths.shape[0]
    for pi in range(pairs):
        first, second = own[2 * pi], own[2 * pi + 1]
        both, lhs, rhs = boths.at[pi], lefts.at[pi], sources.at[pi]
        fill_left(lhs, [left_env.at[lax.div(n, per_left)] for n in (first, second)], wide)
        for pair in range(phys // 2):
            cols = slice(pair * lane, (pair + 1) * lane)
            tiles = two_in_lanes(vec[first, :, cols].astype(F32), vec[second, :, cols].astype(F32))
            for half, tile in enumerate(tiles):
                s = 2 * pair + half
                both[:, s * lane : (s + 1) * lane] = tile.astype(BF)
                put_source(rhs, s, tile)
    for pi in range(pairs):
        contract_left(lefts.at[pi], 0, sources.at[pi], con)
        mix(amat, con, mixes.at[pi], phys, lane)


def quarter_of(place, k, rows):
    return pl.multiple_of(lax.bitwise_xor(place[0], k) * rows, rows)


def right_kernel(terms, kinds, wide, phys, place, mixes, boths, *refs):
    pairs = len(kinds)
    count = len({at for pair in kinds for at, _ in pair})
    rights, refs = refs[:count], refs[count:]
    images, line, rmats = refs[:3]
    outs, accs = refs[3 : 3 + terms], refs[3 + terms]
    lane = 2 * wide
    slab = wide // terms
    at = lax.broadcasted_iota(jnp.int32, (1, lane), 1)
    row = jnp.zeros((1, lane), F32)
    for pi in range(pairs):
        fill_right(rmats.at[pi], tiles_of(rights, kinds[pi], lane), lane)
    for pi in range(pairs):
        contract_right(mixes.at[pi], rmats.at[pi], accs.at[pi])
    for pi in range(pairs):
        both, image, acc = boths.at[pi], images.at[pi], accs.at[pi]
        norm = jnp.zeros((wide, lane), F32)
        corr = jnp.zeros((wide, lane), F32)
        for y in range(phys):
            cols = slice(y * lane, (y + 1) * lane)
            tile = acc[pl.ds(y, wide, stride=phys), :].astype(BF)
            image[:, cols] = tile
            value = tile.astype(F32)
            vec = both[:, cols].astype(F32)
            norm += vec * vec
            corr += vec * value
        norm = jnp.sum(norm, keepdims=True)
        corr = jnp.sum(corr, keepdims=True)
        ratio = jnp.where(norm > 0, corr / jnp.where(norm > 0, norm, 1.0), 0.0)
        square = jnp.zeros((wide, lane), F32)
        cross = jnp.zeros((wide, lane), F32)
        for y in range(phys):
            cols = slice(y * lane, (y + 1) * lane)
            vec = both[:, cols].astype(F32)
            rest = image[:, cols].astype(F32) - ratio * vec
            square += rest * rest
            cross += rest * vec
        square = jnp.sum(square, keepdims=True)
        cross = jnp.sum(cross, keepdims=True)
        for i, value in enumerate((norm, corr, ratio, square, cross)):
            row = jnp.where(at == SUMS * pi + i, value, row)
        for k, out in enumerate(outs):
            out[pi] = image[pl.ds(quarter_of(place, k, slab), slab), :]
    line[...] = jnp.broadcast_to(row[None], line.shape)


def tiles_of(rights, kind, lane):
    return [
        lambda pair, ref=rights[array], at=at: ref[at, :, pair * lane : (pair + 1) * lane]
        for array, at in kind
    ]


def scalars(everyone, pairs):
    def all_of(i):
        return [everyone[:, SUMS * pi + i : SUMS * pi + i + 1] for pi in range(pairs)]

    def total(columns):
        return jnp.sum(functools.reduce(jnp.add, columns), keepdims=True)

    norm_sq = total(all_of(0))
    ratio = total(all_of(1)) / norm_sq
    rests = []
    for norm, own, square, cross in zip(*(all_of(i) for i in (0, 2, 3, 4))):
        off = own - ratio
        rests.append(square + 2 * off * cross + off * off * norm)
    return ratio, jnp.sqrt(norm_sq / (total(rests) + 1e-06))


def product_rows(place, chip, lhs, rhs, amat, rmat, outs, scratch, phys):
    con, mixed, acc = scratch
    lane = acc.shape[1]
    slab = outs[0].shape[0]
    other = lax.bitwise_xor(lax.div(place[0], 2), chip)
    contract_left(lhs, other * con.shape[0], rhs, con)
    mix(amat, con, mixed, phys, lane)
    contract_right(mixed, rmat, acc)
    for k, out in enumerate(outs):
        at = lax.rem(lax.bitwise_xor(place[0], k), 2) * slab * phys
        for y in range(phys):
            out[:, y * lane : (y + 1) * lane] = acc[pl.ds(at + y, slab, stride=phys), :].astype(BF)


def far_kernel(terms, pi, phys, place, everyone, boths, images, lefts, amat, rmats, *refs):
    far = terms - 2
    carried = refs[:far] if pi == 0 else ()
    outs = refs[len(carried) : len(carried) + far]
    rhs, *scratch = refs[len(carried) + far :]
    lane = boths.shape[2] // phys
    ratio, scale = scalars(everyone, boths.shape[0])
    for s in range(phys):
        cols = slice(s * lane, (s + 1) * lane)
        rest = images[pi, :, cols].astype(F32) - ratio * boths[pi, :, cols].astype(F32)
        put_source(rhs, s, (rest * scale).astype(BF).astype(F32))
    for out, piece in zip(outs, carried):
        out[: piece.shape[0]] = piece[...]
    last = outs[0].shape[0] - 1
    for chip in range(1, terms // 2):
        both = [outs[2 * chip - 2 + k].at[last] for k in range(2)]
        product_rows(place, chip, lefts.at[pi], rhs, amat, rmats.at[pi], both, scratch, phys)


def near_kernel(pairs, phys, place, lefts, amat, rmats, *refs):
    sources, outs, scratch = refs[:pairs], refs[pairs : 2 * pairs + 1], refs[2 * pairs + 1 :]
    for pi in range(pairs):
        both = [outs[0].at[pi], outs[1 + pi].at[0]]
        product_rows(
            place, 0, lefts.at[pi], sources[pi], amat, rmats.at[pi], both, scratch, phys
        )


def select_kernel(wide, blocks, names, asked, right_env, *refs):
    outs = refs[:-2]
    spread, rows_out = refs[-2:]
    env_width = right_env.shape[1]
    lane = 2 * wide
    half = wide // 2
    groups = outs[0].shape[2] // wide
    for i, (out, at) in enumerate(blocks):
        env = right_env.at[asked[i]]
        for z in range(half):
            tile = env[:, z * lane : (z + 1) * lane].astype(F32)
            for top in range(0, env_width, 8):
                part = tile[top : top + 8]
                base = top * half + z * 8
                spread[base : base + part.shape[0], :] = part

        def rows_of(g):
            name = names[g]
            return spread[pl.ds((name // 8) * (8 * half) + name % 8, half, stride=8), :]

        for pair in range(groups // 2):
            even, odd = two_in_lanes(rows_of(2 * pair), rows_of(2 * pair + 1))
            rows_out[pl.ds(0, half, stride=2), :] = even
            rows_out[pl.ds(1, half, stride=2), :] = odd
            outs[out][at, :, pair * lane : (pair + 1) * lane] = rows_out[...].astype(BF)


def place_kernel(terms, wide, phys, count, follows, table, *refs):
    if follows:
        ratio, scale = scalars(refs[0], count)
        vec, refs = refs[1], refs[2:]
        out, following = refs[-2:]
    else:
        out = refs[-1]
    lane = 2 * wide
    blocks, slab, _ = out.shape
    slots = blocks // terms
    me = table[blocks]
    for k in range(terms):
        source = lax.bitwise_xor(me, k)
        for pi in range(count):
            if not follows and k == 1:
                piece = refs[k][pi].at[0]
            elif follows or k < 2:
                piece = refs[k].at[pi]
            elif pi == 0:
                piece = refs[k].at[count]
            else:
                piece = refs[terms + (pi - 1) * (terms - 2) + k - 2].at[0]
            first = table[source * slots + 2 * pi]
            second = table[source * slots + 2 * pi + 1]
            for pair in range(phys // 2):
                cols = slice(pair * lane, (pair + 1) * lane)
                both = two_in_lanes(
                    piece[:, 2 * pair * lane : (2 * pair + 1) * lane].astype(F32),
                    piece[:, (2 * pair + 1) * lane : (2 * pair + 2) * lane].astype(F32),
                )
                for where, value in zip((first, second), both):
                    out[where, :, cols] = value.astype(BF)
                    if follows:
                        rows = pl.ds(pl.multiple_of(me * slab, slab), slab)
                        rest = value - ratio * vec[where, rows, cols].astype(F32)
                        following[where, :, cols] = (rest * scale).astype(BF)


def place_all(terms, wide, phys, count, table, everyone, vec, own_first, chip_first, own, *refs):
    others, (first, following, second) = refs[:-3], refs[-3:]
    far, chip = others[:-count], others[-count:]
    ahead = (own_first, chip_first, *far[: terms - 2])
    place_kernel(terms, wide, phys, count, True, table, everyone, vec, *ahead, first, following)
    place_kernel(terms, wide, phys, count, False, table, own, chip, *far, second)


def call(kernel, tables, operands, out_shapes, scratch, flops, moved):
    specs = [
        pl.BlockSpec(memory_space=pltpu.SMEM if i < tables else pltpu.VMEM)
        for i in range(len(operands))
    ]
    return pl.pallas_call(
        kernel,
        out_shape=out_shapes,
        in_specs=specs,
        out_specs=[pl.BlockSpec(memory_space=pltpu.VMEM)] * len(out_shapes),
        scratch_shapes=scratch,
        compiler_params=pltpu.CompilerParams(vmem_limit_bytes=VMEM_LIMIT),
        cost_estimate=pl.CostEstimate(flops=flops // 64, bytes_accessed=moved // 64, transcendentals=0),
    )(*operands)


def body(vector, right_sector, left_env, right_env, term_ops, term_left, group_right):
    terms = lax.axis_size("term")
    secs = lax.axis_size("sec")
    per_device, per_left, wide, row_width = vector.shape
    phys = row_width // wide
    lane = 2 * wide
    blocks = per_device * per_left
    slots = blocks // terms
    pairs = slots // 2
    span = secs // terms
    each = blocks // secs
    env_width = left_env.shape[1]
    depth = -(-env_width // 16) * 16
    local = group_right.shape[0]
    groups = local * terms
    slab = wide // terms
    d = lax.axis_index("sec")
    me = lax.axis_index("term")
    both_axes = ("sec", "term")
    vec = vector.reshape(blocks, wide, row_width)

    lines = terms // 2

    def flip(t, a):
        return (2 * a + (t + a) % 2) * lines + t // 2

    flat = right_sector.reshape(blocks)
    dest = flat // per_device
    before = jnp.arange(blocks)[None, :] < jnp.arange(blocks)[:, None]
    rank = jnp.sum((dest[None, :] == dest[:, None]) & before, axis=1)
    flips = dest ^ d
    a = flips // lines // 2
    t = flips % lines * 2 + (flips // lines + a) % 2
    place = t * slots + a * each + rank
    hit = place[None, :] == jnp.arange(blocks)[:, None]
    order = jnp.sum(jnp.where(hit, jnp.arange(blocks)[None, :], 0), axis=1)
    by_place = jnp.sum(jnp.where(hit, (flat % per_device)[None, :], 0), axis=1)
    own = lax.dynamic_slice(order, (me * slots,), (slots,)).astype(jnp.int32)
    wanted = lax.dynamic_slice(by_place, (me * slots,), (slots,)).astype(jnp.int32)
    table = jnp.concatenate([order.astype(jnp.int32), me.reshape(1)])

    swaps = [
        [(e * terms + t, (e ^ flip(t, a)) * terms + t) for e in range(secs) for t in range(terms)]
        for a in range(span)
    ]
    asked = [
        lax.ppermute(wanted[a * each : (a + 1) * each], both_axes, swaps[a]) for a in range(span)
    ]

    onehot = (term_left[:, :, None] == jnp.arange(depth)).astype(BF)
    operator = jnp.einsum(
        "gtys,gtw->gysw", term_ops, onehot, preferred_element_type=F32
    ).reshape(local * phys, phys * depth)
    names = jnp.pad(
        group_right.astype(F32)[None, :], ((0, 15), (0, phys * depth - local))
    )
    packed = jnp.concatenate([operator, names], axis=0).astype(BF)

    def shift(value, k):
        return lax.ppermute(value, "term", [(t, t ^ k) for t in range(terms)])

    parts = [packed] + [shift(packed, k) for k in range(1, terms)]
    known = jnp.concatenate([p[local * phys, :local] for p in parts]).astype(jnp.int32)
    asked = jnp.concatenate(asked)

    right_shape = jax.ShapeDtypeStruct((each, wide, groups * wide), BF)
    chosen = call(
        functools.partial(select_kernel, wide, [(i // each, i % each) for i in range(slots)]),
        2,
        (known, asked, right_env),
        [right_shape] * span,
        [
            pltpu.VMEM((-(-env_width // 8) * 8 * (wide // 2), lane), F32),
            pltpu.VMEM((wide, lane), F32),
        ],
        0,
        slots * env_width * wide * wide * 2,
    )
    rights = [lax.ppermute(chosen[a], both_axes, swaps[a]) for a in range(span)]
    left_env, _ = lax.optimization_barrier((left_env, chosen))

    rows = wide * depth
    left_flops = 2 * rows * 4 * wide * phys * lane
    mix_flops = 2 * groups * phys * phys * depth * wide * lane
    right_flops = 2 * wide * phys * groups * lane * lane

    def stacked(*shape):
        return jax.ShapeDtypeStruct(shape, BF)

    mixed_shape = (wide * phys, groups * lane)
    rhs_scratch = pltpu.VMEM((4 * wide, phys * lane), BF)
    con_scratch = pltpu.VMEM((rows, phys * lane), BF)
    acc_scratch = pltpu.VMEM((wide * phys, lane), F32)
    mixes, boths, lefts, amat = call(
        functools.partial(left_kernel, per_left, wide, phys),
        1,
        (own, left_env, vec, *parts),
        [
            stacked(pairs, *mixed_shape),
            stacked(pairs, wide, phys * lane),
            stacked(pairs, rows, 4 * wide),
            stacked(groups * phys, phys * depth),
        ],
        [pltpu.VMEM((pairs, 4 * wide, phys * lane), BF), con_scratch],
        pairs * (left_flops + mix_flops),
        pairs * wide * phys * groups * lane * 2,
    )

    where = me.reshape(1).astype(jnp.int32)
    kinds = [[((2 * pi + b) // each, (2 * pi + b) % each) for b in range(2)] for pi in range(pairs)]
    images, line, rmats, *pieces = call(
        functools.partial(right_kernel, terms, kinds, wide, phys),
        1,
        (where, mixes, boths, *rights),
        [
            stacked(pairs, wide, phys * lane),
            jax.ShapeDtypeStruct((secs * terms, 1, lane), F32),
            stacked(pairs, lane, groups * lane),
        ]
        + [stacked(pairs, slab, phys * lane)] * terms,
        [pltpu.VMEM((pairs, wide * phys, lane), F32)],
        pairs * right_flops,
        pairs * wide * phys * groups * lane * 2,
    )

    everyone = lax.all_to_all(line, both_axes, 0, 0, tiled=True).reshape(-1, lane)
    pieces, everyone = lax.optimization_barrier((pieces, everyone))

    part_scratch = [
        pltpu.VMEM((2 * slab * depth, phys * lane), BF),
        pltpu.VMEM((2 * slab * phys, groups * lane), BF),
        pltpu.VMEM((2 * slab * phys, lane), F32),
    ]
    product_flops = left_flops + mix_flops + right_flops
    far_pieces, sources, sums = [], [], everyone
    for pi in range(pairs):
        carried = pieces[2:] if pi == 0 else []
        *outs, source = call(
            functools.partial(far_kernel, terms, pi, phys),
            1,
            (where, sums, boths, images, lefts, amat, rmats, *carried),
            [stacked(pairs + 1 if carried else 1, slab, phys * lane)] * (terms - 2)
            + [stacked(4 * wide, phys * lane)],
            part_scratch,
            product_flops * (terms - 2) // terms,
            4 * wide * phys * lane * 2,
        )
        outs, sums = lax.optimization_barrier((outs, sums))
        far_pieces.append([shift(out, k + 2) for k, out in enumerate(outs)])
        sources.append(source)
    near_pieces = call(
        functools.partial(near_kernel, pairs, phys),
        1,
        (where, lefts, amat, rmats, *sources),
        [stacked(pairs, slab, phys * lane)] + [stacked(1, slab, phys * lane)] * pairs,
        part_scratch,
        pairs * product_flops * 2 // terms,
        4 * wide * phys * lane * 2,
    )
    near_pieces = [near_pieces[0]] + [shift(piece, 1) for piece in near_pieces[1:]]

    out_shape = jax.ShapeDtypeStruct((blocks, slab, row_width), BF)
    far = [piece for one_pair in far_pieces for piece in one_pair]
    first_image, next_rows, second_image = call(
        functools.partial(place_all, terms, wide, phys, pairs),
        1,
        (table, everyone, vec, pieces[0], shift(pieces[1], 1), near_pieces[0], *far, *near_pieces[1:]),
        [out_shape] * 3,
        [],
        0,
        blocks * slab * row_width * 12,
    )
    shape = (per_device, per_left, slab, row_width)
    return (first_image.reshape(shape), next_rows.reshape(shape), second_image.reshape(shape))


def solution(mesh):
    in_specs = (
        P("sec", None, None, None),
        P("sec", None),
        P("sec", None, None),
        P("sec", None, None),
        P("term", None, None, None),
        P("term", None),
        P("term"),
    )
    out_specs = (
        P("sec", None, "term", None),
        P("sec", None, "term", None),
        P("sec", None, "term", None),
    )
    return jax.shard_map(body, mesh=mesh, in_specs=in_specs, out_specs=out_specs, check_vma=False)
```
